256 devices in a mesh: phi: 16 (over x_hi, z), row: 4 (over x_lo, core), mass: 4 (over y).
Axes of the slice: x: 4 (x_hi: 2, x_lo: 2; x = x_hi * 2 + x_lo), y: 4, z: 8, core: 2. Of those that a mesh axis runs over, the one named last changes fastest.
Arguments:
- density: float32 [256, 512, 512], P('mass', 'phi', 'row'), may hold values from 0.05 to 1
- cotangent: float32 [256, 512, 512], P('mass', 'phi', 'row'), may hold values from -6 to 6
- drift_in: float32 [256, 512], P('mass'), may hold values from 0.02 to 0.3
- drift_out: float32 [256, 512], P('mass'), may hold values from 0.02 to 0.3
- spread: float32 [256], P('mass'), may hold values from 0.01 to 0.15
- dest_bins: int32 [256], replicated, may hold values from 1 to 254, as said below
- bott_split: float32 [256], replicated, may hold values from 0.05 to 0.95
- coag_rate: float32 [256], replicated, may hold values from 0.05 to 0.3
- frag_pairs: int32 [4, 4], replicated, may hold values from 0 to 1, as said below
- frag_gain: float32 [256, 256], replicated, may hold values from 0.001 to 0.02
- frag_rate: float32 [256], replicated, may hold values from 0.02 to 0.2
- collide_speed: float32 [512, 512], P('phi', 'row'), may hold values from 0.2 to 5
- frag_speed: float32 [512], P('row'), may hold values from 0.5 to 2
- regime: int32 [512, 512], P('phi', 'row'), may hold values 0 or 1
Outputs:
- density_adjoint: float32 [256, 512, 512], P('mass', 'phi', 'row')
- speed_gradient: float32 [512], P('row')
The draws below stay inside these ranges and needn't reach their ends.
Inputs may be any that keep to these rules, and one draw needn't show every extreme that they name: dest_bins[j] lies between j + 1 and j + 6, but never above 254; dest_bins[0] is 1 and the top bins map to 254. frag_pairs is 1 on the diagonal and in the first row, 0 below the diagonal.
All inputs are finite; a program needn't handle non-finite values. No bound on the sum of `regime` on one device may be relied on, other than what follows from the above.
Results may differ from the reference program's by a relative error of at most 0.000078.
Values sent between devices are 32-bit elements; how exact they have to be, the bound alone decides.
A program may use at most 128 MiB of HBM per device.

```python
import math
import jax
import jax.numpy as jnp
from jax import lax

MB = 256
RANGE = 64
NB = 4
NA = 512
NR = 512


def draw_dest_bins(key, part):
    offsets = jax.random.randint(key, (MB,), 0, 6, dtype=jnp.int32)
    bin_ids = jnp.arange(MB, dtype=jnp.int32)
    offsets = jnp.where(bin_ids == 0, 0, offsets)
    return jnp.minimum(bin_ids + 1 + offsets, MB - 2).astype(jnp.int32)


def draw_frag_pairs(key, part):
    source_ids = jnp.arange(NB, dtype=jnp.int32)[None, :]
    target_ids = jnp.arange(NB, dtype=jnp.int32)[:, None]
    random_bits = jax.random.randint(key, (NB, NB), 0, 2, dtype=jnp.int32)
    always_on = jnp.logical_or(target_ids == source_ids, target_ids == 0)
    chosen = jnp.where(always_on, 1, random_bits)
    return jnp.where(source_ids < target_ids, 0, chosen).astype(jnp.int32)


def set_ends(array, own_key, low, high):
    spot = [jax.random.randint(jax.random.fold_in(own_key, axis), (), 0, length) for axis, length in enumerate(array.shape)]
    longest = array.shape.index(max(array.shape))
    next_to = spot[:longest] + [(spot[longest] + 1) % array.shape[longest]] + spot[longest + 1:]
    return array.at[tuple(spot)].set(low).at[tuple(next_to)].set(high)


def shard_levels(stream_key, extent, cuts, least, high):
    factor_of = 1.0
    for dim, blocks in cuts:
        draws = jax.random.uniform(jax.random.fold_in(jax.random.fold_in(stream_key, 6), dim), (blocks,), jnp.float32, least / len(cuts), high / len(cuts))
        factor_of = factor_of * jnp.repeat(jnp.exp(draws), extent[dim] // blocks).reshape((-1,) + (1,) * (len(extent) - 1 - dim))
    return factor_of


def normal_values(own_key, dims, deviation, bound, shards=(), kind=jnp.bfloat16):
    result = jax.random.normal(own_key, dims, jnp.float32) * deviation
    if len(shards) > 0:
        result = shard_levels(own_key, dims, shards, -0.22, 0.18) * result
    return jnp.clip(result, min=-bound, max=bound).astype(kind)


def setup_inputs(seed: int = 0) -> dict:
    splits = jax.random.split(jax.random.key(seed), 15)
    return {
        "density": jnp.clip(jnp.exp(math.log(1.0) - 2.9957323 * jax.random.uniform(splits[0], (MB, NA, NR), jnp.float32) ** shard_levels(splits[0], (MB, NA, NR), ((0, 4), (1, 16), (2, 4)), -0.2, 0.2)), 0.05, 1.0),
        "cotangent": normal_values(splits[1], (MB, NA, NR), 1.0, 6.0, ((0, 4), (1, 16), (2, 4)), jnp.float32),
        "drift_in": jnp.clip(jnp.exp(math.log(0.3) - 2.7080503 * jax.random.uniform(splits[2], (MB, NR), jnp.float32) ** shard_levels(splits[2], (MB, NR), ((0, 4),), -0.2, 0.2)), 0.02, 0.3),
        "drift_out": jnp.clip(jnp.exp(math.log(0.3) - 2.7080503 * jax.random.uniform(splits[3], (MB, NR), jnp.float32) ** shard_levels(splits[3], (MB, NR), ((0, 4),), -0.2, 0.2)), 0.02, 0.3),
        "spread": jnp.clip(jnp.exp(math.log(0.15) - 2.7080503 * jax.random.uniform(splits[4], (MB,), jnp.float32) ** shard_levels(splits[4], (MB,), ((0, 4),), -0.2, 0.2)), 0.01, 0.15),
        "dest_bins": draw_dest_bins(jax.random.fold_in(splits[14], 71), 0),
        "bott_split": jnp.clip(jax.random.uniform(splits[6], (MB,), jnp.float32, 0.05, 0.95), 0.05, 0.95),
        "coag_rate": jnp.clip(jnp.exp(jax.random.uniform(splits[7], (MB,), jnp.float32, math.log(0.05), math.log(0.3))), 0.05, 0.3),
        "frag_pairs": draw_frag_pairs(jax.random.fold_in(splits[14], 71), 0),
        "frag_gain": jnp.clip(jnp.exp(jax.random.uniform(splits[9], (MB, MB), jnp.float32, math.log(0.001), math.log(0.02))), 0.001, 0.02),
        "frag_rate": jnp.clip(jnp.exp(jax.random.uniform(splits[10], (MB,), jnp.float32, math.log(0.02), math.log(0.2))), 0.02, 0.2),
        "collide_speed": jnp.clip(jnp.exp(math.log(5.0) - 3.218876 * jax.random.uniform(splits[11], (NA, NR), jnp.float32) ** shard_levels(splits[11], (NA, NR), ((0, 16), (1, 4)), -0.2, 0.2)), 0.2, 5.0),
        "frag_speed": jnp.clip(0.5 + 1.5 * jax.random.uniform(splits[12], (NR,), jnp.float32) ** shard_levels(splits[12], (NR,), ((0, 4),), -0.2, 0.2), 0.5, 2.0),
        "regime": set_ends((jax.random.randint(splits[13], (NA, NR), 0, 4) < 3).astype(jnp.int32), jax.random.fold_in(splits[13], 1), 0, 1),
    }


gate_width = 0.5
highest = lax.Precision.HIGHEST


def coag_matrix(dest_bins, bott_split, coag_rate):
    number = dest_bins.shape[0]
    row_ids = jnp.arange(number, dtype=jnp.int32)[:, None]
    col_ids = jnp.arange(number, dtype=jnp.int32)[None, :]
    target = dest_bins[None, :]
    lower_part = (row_ids == target).astype(jnp.float32) * (1.0 - bott_split)[None, :]
    upper_part = (row_ids == target + 1).astype(jnp.float32) * bott_split[None, :]
    keeper = (row_ids == col_ids).astype(jnp.float32)
    return (lower_part + upper_part - keeper) * coag_rate[None, :]


def frag_matrix(frag_pairs, frag_gain, frag_rate):
    number = frag_gain.shape[0]
    blocks = jnp.repeat(jnp.repeat(frag_pairs, RANGE, axis=0), RANGE, axis=1).astype(jnp.float32)
    row_ids = jnp.arange(number, dtype=jnp.int32)[:, None]
    col_ids = jnp.arange(number, dtype=jnp.int32)[None, :]
    below_diag = (row_ids <= col_ids).astype(jnp.float32)
    keeper = (row_ids == col_ids).astype(jnp.float32)
    return frag_gain * blocks * below_diag - keeper * frag_rate[None, :]


def transport(field, drift_in, drift_out, spread):
    center = 1.0 - drift_in - drift_out - 2.0 * spread[:, None]
    padded = jnp.pad(field, ((0, 0), (0, 0), (1, 1)))
    in_pad = jnp.pad(drift_in, ((0, 0), (1, 1)))
    out_pad = jnp.pad(drift_out, ((0, 0), (1, 1)))
    beside_all = jnp.roll(field, 1, axis=1) + jnp.roll(field, -1, axis=1)
    return (center[:, None, :] * field + in_pad[:, None, 2:] * padded[:, :, 2:]
            + out_pad[:, None, :-2] * padded[:, :, :-2] + spread[:, None, None] * beside_all)


def transport_back(field, drift_in, drift_out, spread):
    center = 1.0 - drift_in - drift_out - 2.0 * spread[:, None]
    padded = jnp.pad(field, ((0, 0), (0, 0), (1, 1)))
    beside_all = jnp.roll(field, 1, axis=1) + jnp.roll(field, -1, axis=1)
    return (center[:, None, :] * field + drift_in[:, None, :] * padded[:, :, :-2]
            + drift_out[:, None, :] * padded[:, :, 2:] + spread[:, None, None] * beside_all)


def bins_apply(matrix, field):
    layout = field.shape
    flat_field = field.reshape(layout[0], -1)
    return jnp.dot(matrix, flat_field, precision=highest, preferred_element_type=jnp.float32).reshape(layout)


def reference(density, cotangent, drift_in, drift_out, spread, dest_bins, bott_split, coag_rate, frag_pairs, frag_gain, frag_rate, collide_speed, frag_speed, regime):
    coag_full = coag_matrix(dest_bins, bott_split, coag_rate)
    frag_full = frag_matrix(frag_pairs, frag_gain, frag_rate)
    sigma = jax.nn.sigmoid((collide_speed - frag_speed[None, :]) / gate_width)
    flagged = regime.astype(jnp.float32)
    frag_gate = flagged * sigma
    gate_slope = -flagged * sigma * (1.0 - sigma) / gate_width
    moved_first = transport(density, drift_in, drift_out, spread)
    mixed_first = bins_apply(coag_full, moved_first) + bins_apply(frag_full, frag_gate[None] * moved_first)
    state_first = moved_first + mixed_first
    moved_second = transport(state_first, drift_in, drift_out, spread)
    coag_second = bins_apply(coag_full.T, cotangent)
    frag_second = bins_apply(frag_full.T, cotangent)
    weight_second = cotangent + (coag_second + frag_gate[None] * frag_second)
    adjoint_first = transport_back(weight_second, drift_in, drift_out, spread)
    coag_first = bins_apply(coag_full.T, adjoint_first)
    frag_first = bins_apply(frag_full.T, adjoint_first)
    weight_first = adjoint_first + (coag_first + frag_gate[None] * frag_first)
    density_adjoint = transport_back(weight_first, drift_in, drift_out, spread)
    products = jnp.sum(moved_first * frag_first + moved_second * frag_second, axis=0)
    speed_gradient = jnp.sum(gate_slope * products, axis=0)
    return density_adjoint, speed_gradient
```

```python
import functools

import jax
import jax.numpy as jnp
from jax import lax
from jax.experimental import pallas as pl
from jax.experimental.pallas import tpu as pltpu
from jax.sharding import PartitionSpec as P


MESH = pl.DeviceIdType.MESH
F32 = jnp.float32
BF16 = jnp.bfloat16
RANGE = 64
MASS = 4
ROWS = 8
BINS = 256
LANES = 128
GATE_WIDTH = 0.5
BACK, FORTH = 0, 1


def lanes_of(shape):
    return lax.broadcasted_iota(jnp.int32, shape, len(shape) - 1)


def rolled(value, shift):
    shift = shift % LANES
    return value if shift == 0 else pltpu.roll(value, shift, value.ndim - 1)


def swap_blocks(tiles):
    block = lanes_of(tiles[0].shape) // 32
    low = block < 2
    even = block % 2 == 0
    s0, s1, s2, s3 = tiles
    a0 = jnp.where(low, s0, rolled(s2, 64))
    a2 = jnp.where(low, rolled(s0, 64), s2)
    a1 = jnp.where(low, s1, rolled(s3, 64))
    a3 = jnp.where(low, rolled(s1, 64), s3)
    return (
        jnp.where(even, a0, rolled(a1, 32)),
        jnp.where(even, rolled(a0, 96), a1),
        jnp.where(even, a2, rolled(a3, 32)),
        jnp.where(even, rolled(a2, 96), a3),
    )


def high_low(value):
    high = value.astype(BF16)
    return high, (value - high.astype(F32)).astype(BF16)


def kernel(
    pairs,
    density,
    cotangent,
    drift_in,
    drift_out,
    spread,
    dest,
    split,
    rate,
    gain,
    frag_rate,
    speed,
    frag_speed,
    regime,
    out,
    grad,
    raw_c,
    raw_d,
    pack_c,
    pack_d,
    cot,
    dens,
    coef_out,
    coef_in,
    coef,
    back_hi,
    back_lo,
    forth_hi,
    forth_lo,
    gates,
    slopes,
    w2,
    f2,
    a1,
    w1,
    f1,
    m1,
    st,
    res,
    ret,
    edge_out,
    edge_in,
    acc,
    red,
    load_sem,
    field_send,
    field_recv,
    coef_send,
    coef_recv,
    edge_send,
    edge_recv,
    red_send,
    red_recv,
):
    phi = lax.axis_index("phi")
    row = lax.axis_index("row")
    m = lax.axis_index("mass")
    phis = lax.axis_size("phi")
    rows = lax.axis_size("row")
    phi_j = lax.rem(phi, 4)
    phi_i = phi // 4

    load_c = pltpu.make_async_copy(cotangent, raw_c, load_sem.at[0])
    load_d = pltpu.make_async_copy(density, raw_d, load_sem.at[1])
    load_c.start()
    load_d.start()

    def mass_peer(k):
        return {"mass": lax.rem(m + k, MASS)}

    def j_peer(k):
        return {"phi": phi_i * 4 + lax.rem(phi_j + k, 4)}

    def i_peer(k):
        return {"phi": lax.rem(phi_i + k, 4) * 4 + phi_j}

    radial = row * MASS + m
    radials = rows * MASS
    right_at = lax.rem(radial + 1, radials)
    left_at = lax.rem(radial + radials - 1, radials)
    right = {"row": right_at // MASS, "mass": lax.rem(right_at, MASS)}
    left = {"row": left_at // MASS, "mass": lax.rem(left_at, MASS)}
    after = {"phi": lax.rem(phi + 1, phis)}
    before = {"phi": lax.rem(phi + phis - 1, phis)}

    barrier = pltpu.get_barrier_semaphore()
    greeted = (
        [mass_peer(k) for k in (1, 2, 3)]
        + [j_peer(k) for k in (1, 2, 3)]
        + [i_peer(k) for k in (1, 2, 3)]
        + [right, left, after, before]
    )
    for device in greeted:
        pl.semaphore_signal(barrier, inc=1, device_id=device, device_id_type=MESH)

    tile = (RANGE, LANES)
    lane = lanes_of(tile)
    block = lane // 32
    within = lax.rem(lane, 32)
    first = within == 0
    final = within == 31
    at = pl.multiple_of(row * LANES, LANES)
    in_q = drift_in[:, pl.ds(at, LANES)]
    out_q = drift_out[:, pl.ds(at, LANES)]
    square = (RANGE, RANGE)
    on_diag = lax.broadcasted_iota(jnp.int32, square, 0) == lanes_of(square)
    spread_col = jnp.sum(jnp.where(on_diag, jnp.broadcast_to(spread[...], square), 0.0), axis=1, keepdims=True)
    spread_tile = jnp.broadcast_to(spread_col, tile)
    for k in range(MASS):
        coef_out[k] = jnp.where(
            block == 0,
            rolled(in_q, -32 * k),
            jnp.where(block == 1, rolled(out_q, 32 - 32 * k), spread_tile),
        )

    def field_copy(kind, k, ah, source, target):
        return pltpu.make_async_remote_copy(
            src_ref=source,
            dst_ref=target,
            send_sem=field_send.at[kind, k - 1, ah],
            recv_sem=field_recv.at[kind, k - 1, ah],
            device_id=mass_peer(k),
            device_id_type=MESH,
        )

    own = pl.ds(pl.multiple_of(m * RANGE, RANGE), RANGE)

    def cot_copy(k, ah):
        return field_copy(0, k, ah, pack_c.at[lax.rem(m + k, MASS), ah], cot.at[ah, own])

    def dens_copy(k, ah):
        return field_copy(1, k, ah, pack_d.at[lax.rem(m + k, MASS), ah], dens.at[ah + 1, own])

    def ret_copy(k, ah):
        theirs = pl.ds(pl.multiple_of(lax.rem(m + k, MASS) * RANGE, RANGE), RANGE)
        return field_copy(2, k, ah, res.at[ah, theirs], ret.at[m, ah])

    def coef_copy(k):
        return pltpu.make_async_remote_copy(
            src_ref=coef_out.at[lax.rem(m + k, MASS)],
            dst_ref=coef_in.at[own],
            send_sem=coef_send.at[k - 1],
            recv_sem=coef_recv.at[k - 1],
            device_id=mass_peer(k),
            device_id_type=MESH,
        )

    def spread_field(raw, packed, shifted, held, copy):
        flat = raw.reshape(RANGE * 32, LANES)

        def body(ah, carry):
            tiles = swap_blocks([flat[pl.ds(al * 8 + ah, RANGE, stride=32), :] for al in range(4)])
            for k in range(MASS):
                packed[k, ah] = tiles[k]
            for k in (1, 2, 3):
                copy(k, ah).start()
            held[ah + shifted, own] = packed[m, ah]
            return carry

        lax.fori_loop(0, ROWS, body, 0)

    load_c.wait()
    pl.semaphore_wait(barrier, len(greeted))
    spread_field(raw_c, pack_c, 0, cot, cot_copy)
    for k in (1, 2, 3):
        coef_copy(k).start()
    coef_in[own] = coef_out[m]
    load_d.wait()
    spread_field(raw_d, pack_d, 1, dens, dens_copy)

    whole = (BINS, BINS)
    row_ids = lax.broadcasted_iota(jnp.int32, whole, 0)
    col_ids = lanes_of(whole)
    target = jnp.broadcast_to(dest[...], whole)
    upper = jnp.broadcast_to(split[...], whole)
    diag = jnp.where(row_ids == col_ids, 1.0, 0.0)
    coag_full = (
        jnp.where(row_ids == target, 1.0 - upper, 0.0) + jnp.where(row_ids == target + 1, upper, 0.0) - diag
    ) * rate[...]
    strip = (RANGE, BINS)
    strip_block = lanes_of(strip) // RANGE
    chosen = []
    for i in range(MASS):
        line = jnp.zeros(strip, F32)
        for j in range(MASS):
            line = jnp.where(strip_block == j, pairs[i, j].astype(F32), line)
        chosen.append(line)
    chosen = jnp.concatenate(chosen, axis=0)
    frag_full = gain[...] * chosen * jnp.where(row_ids <= col_ids, 1.0, 0.0) - diag * frag_rate[...]
    for at_row, matrix in ((0, coag_full), (BINS, frag_full)):
        hi, lo = high_low(matrix)
        forth_hi[at_row : at_row + BINS] = hi
        forth_lo[at_row : at_row + BINS] = lo
        hi, lo = high_low(matrix.T)
        back_hi[at_row : at_row + BINS] = hi
        back_lo[at_row : at_row + BINS] = lo

    sigma = 1.0 / (1.0 + jnp.exp(-((speed[...] - frag_speed[...]) / GATE_WIDTH)))
    flagged = regime[...].astype(F32)
    gate_all = flagged * sigma
    slope_all = -flagged * sigma * (1.0 - sigma) / GATE_WIDTH
    block8 = lanes_of((ROWS, LANES)) // 32
    for source, kept in ((gate_all, gates), (slope_all, slopes)):
        value = jnp.zeros((ROWS, LANES), F32)
        for al in range(4):
            part = pltpu.roll(source[al * 8 : al * 8 + 8], lax.rem(32 * (al + MASS - m), LANES), 1)
            value = jnp.where(block8 == al, part, value)
        kept[...] = value

    for k in (1, 2, 3):
        coef_copy(k).wait_recv()
    for g in range(MASS):
        bins = slice(g * RANGE, (g + 1) * RANGE)
        turns = [rolled(coef_in[bins], 32 * k) for k in range(4)]

        def everywhere(source):
            value = turns[(0 - source) % 4]
            for b in (1, 2, 3):
                value = jnp.where(block == b, turns[(b - source) % 4], value)
            return value

        c_in, c_out, c_spread = everywhere(0), everywhere(1), everywhere(2)
        coef[0, bins] = c_in
        coef[1, bins] = c_out
        coef[2, bins] = c_spread
        coef[3, bins] = 1.0 - c_in - c_out - 2.0 * c_spread

    has_left = jnp.where(radial > 0, 1.0, 0.0)
    has_right = jnp.where(radial < radials - 1, 1.0, 0.0)

    def edge_copies(n):
        def one(i, device):
            return pltpu.make_async_remote_copy(
                src_ref=edge_out.at[n, i],
                dst_ref=edge_in.at[n, i],
                send_sem=edge_send.at[n, i],
                recv_sem=edge_recv.at[n, i],
                device_id=device,
                device_id_type=MESH,
            )

        return [one(0, right), one(1, left), one(2, after), one(3, before)]

    def send_edges(n, field, way):
        def body(ah, carry):
            last_col, first_col = carry
            for g in range(MASS):
                bins = slice(g * RANGE, (g + 1) * RANGE)
                value = field[ah + 1, bins]
                to_left = value * coef[0, bins] if way == FORTH else value
                to_right = value * coef[1, bins] if way == FORTH else value
                last_col = jnp.where(final, to_right, rolled(last_col, -1))
                first_col = jnp.where(first, to_left, rolled(first_col, 1))
            return last_col, first_col

        zero = jnp.zeros(tile, F32)
        for i in (2, 3):
            value = zero
            for g in range(MASS):
                bins = slice(g * RANGE, (g + 1) * RANGE)
                part = rolled(field[ROWS, bins], 32 * (g - 3)) if i == 2 else rolled(field[1, bins], 32 * g)
                value = jnp.where(block == g, part, value)
            edge_out[n, i] = value
        last_col, first_col = lax.fori_loop(0, ROWS, body, (zero, zero))
        edge_out[n, 0] = last_col
        edge_out[n, 1] = first_col
        for copy in edge_copies(n):
            copy.start()

    def stencil(n, field, way, emit, after_row=None):
        for copy in edge_copies(n):
            copy.wait_recv()
        for g in range(MASS):
            bins = slice(g * RANGE, (g + 1) * RANGE)
            field[0, bins] = jnp.where(
                block == 0, rolled(edge_in[n, 2], -32 * g), rolled(field[ROWS, bins], 32)
            )
            field[ROWS + 1, bins] = jnp.where(
                block == 3, rolled(edge_in[n, 3], 32 * (3 - g)), rolled(field[1, bins], -32)
            )

        def body(ah, carry):
            last_col, first_col = carry
            for g in range(MASS):
                bins = slice(g * RANGE, (g + 1) * RANGE)
                value = field[ah + 1, bins]
                beside = field[ah, bins] + field[ah + 2, bins]
                c_in, c_out = coef[0, bins], coef[1, bins]
                if way == FORTH:
                    outer = jnp.where(final, first_col, rolled(c_in * value, -1))
                    inner = jnp.where(first, last_col, rolled(c_out * value, 1))
                    both = outer + inner
                else:
                    inner = jnp.where(first, last_col, rolled(value, 1))
                    outer = jnp.where(final, first_col, rolled(value, -1))
                    both = c_in * inner + c_out * outer
                emit(ah, g, bins, coef[3, bins] * value + both + coef[2, bins] * beside)
                last_col = rolled(last_col, -1)
                first_col = rolled(first_col, 1)
            if after_row is not None:
                after_row(ah)
            return last_col, first_col

        lax.fori_loop(0, ROWS, body, (edge_in[n, 0] * has_left, edge_in[n, 1] * has_right))

    def mix(source, shifted, hi, lo, state, frags, before_pair=None):
        def body(j, carry):
            ah = 2 * j
            if before_pair is not None:
                before_pair(ah)
                before_pair(ah + 1)
            x = jnp.concatenate([source[ah + shifted], source[ah + shifted + 1]], axis=1)
            x_hi, x_lo = high_low(x)
            y = jnp.dot(hi[...], x_hi, preferred_element_type=F32)
            y += jnp.dot(hi[...], x_lo, preferred_element_type=F32)
            y += jnp.dot(lo[...], x_hi, preferred_element_type=F32)
            gate = jnp.concatenate([gates[pl.ds(ah, 1)], gates[pl.ds(ah + 1, 1)]], axis=1)
            new = x + (y[:BINS] + gate * y[BINS:])
            state[ah + 1] = new[:, :LANES]
            state[ah + 2] = new[:, LANES:]
            if frags is not None:
                frags[ah] = y[BINS:, :LANES]
                frags[ah + 1] = y[BINS:, LANES:]
            return carry

        lax.fori_loop(0, ROWS // 2, body, 0)

    def add_product(ah, value, other):
        summed = jnp.sum((value * other).reshape(RANGE // 8, 8, LANES), axis=0)
        acc[...] += slopes[pl.ds(ah, 1)] * summed

    def arrived(copy):
        def wait(ah):
            for k in (1, 2, 3):
                copy(k, ah).wait_recv()

        return wait

    acc[...] = jnp.zeros((8, LANES), F32)

    mix(cot, 0, back_hi, back_lo, w2, f2, arrived(cot_copy))
    send_edges(0, w2, BACK)

    def keep_a1(ah, g, bins, value):
        a1[ah, bins] = value

    stencil(0, w2, BACK, keep_a1)

    mix(a1, 0, back_hi, back_lo, w1, f1)
    send_edges(1, w1, BACK)

    def wait_dens(ah, carry):
        arrived(dens_copy)(ah)
        return carry

    lax.fori_loop(0, ROWS, wait_dens, 0)
    send_edges(2, dens, FORTH)

    def keep_m1(ah, g, bins, value):
        m1[ah, bins] = value
        add_product(ah, value, f1[ah, bins])

    stencil(2, dens, FORTH, keep_m1)
    mix(m1, 0, forth_hi, forth_lo, st, None)
    send_edges(3, st, FORTH)

    def keep_res(ah, g, bins, value):
        res[ah, bins] = value

    def send_row(ah):
        for k in (1, 2, 3):
            ret_copy(k, ah).start()
        ret[m, ah] = res[ah, own]

    stencil(1, w1, BACK, keep_res, send_row)

    def keep_m2(ah, g, bins, value):
        add_product(ah, value, f2[ah, bins])

    stencil(3, st, FORTH, keep_m2)

    total = jnp.sum(acc[...], axis=0, keepdims=True)
    total = total + rolled(total, 32) + rolled(total, 64) + rolled(total, 96)
    total = jnp.broadcast_to(total, (8, LANES))
    total = jnp.where(block8 == m, total, 0.0)
    for n, (place, peer) in enumerate(((phi_j, j_peer), (phi_i, i_peer), (m, mass_peer))):
        red[n, place] = total
        copies = []
        for k in (1, 2, 3):
            copies.append(
                pltpu.make_async_remote_copy(
                    src_ref=red.at[n, place],
                    dst_ref=red.at[n, place],
                    send_sem=red_send.at[n, k - 1],
                    recv_sem=red_recv.at[n, k - 1],
                    device_id=peer(k),
                    device_id_type=MESH,
                )
            )
        for copy in copies:
            copy.start()
        for copy in copies:
            copy.wait()
        total = (red[n, 0] + red[n, 1]) + (red[n, 2] + red[n, 3])
    grad[...] = total

    flat_out = out.reshape(RANGE * 32, LANES)

    def unpack(ah, carry):
        arrived(ret_copy)(ah)
        tiles = swap_blocks([ret[k, ah] for k in range(MASS)])
        for al in range(4):
            flat_out[pl.ds(al * 8 + ah, RANGE, stride=32), :] = tiles[al]
        return carry

    lax.fori_loop(0, ROWS, unpack, 0)

    def drain(ah, carry):
        for copy in (cot_copy, dens_copy, ret_copy):
            for k in (1, 2, 3):
                copy(k, ah).wait_send()
        return carry

    lax.fori_loop(0, ROWS, drain, 0)
    for k in (1, 2, 3):
        coef_copy(k).wait_send()
    for n in range(4):
        for copy in edge_copies(n):
            copy.wait_send()


def per_device(
    density,
    cotangent,
    drift_in,
    drift_out,
    spread,
    dest_bins,
    bott_split,
    coag_rate,
    frag_pairs,
    frag_gain,
    frag_rate,
    collide_speed,
    frag_speed,
    regime,
):
    vmem = pl.BlockSpec(memory_space=pltpu.VMEM)
    hbm = pl.BlockSpec(memory_space=pl.ANY)
    smem = pl.BlockSpec(memory_space=pltpu.SMEM)
    field = pltpu.VMEM((ROWS, BINS, LANES), F32)
    padded = pltpu.VMEM((ROWS + 2, BINS, LANES), F32)
    packed = pltpu.VMEM((MASS, ROWS, RANGE, LANES), F32)
    raw = pltpu.VMEM(density.shape, F32)
    matrix = pltpu.VMEM((2 * BINS, BINS), BF16)
    small = pltpu.VMEM((ROWS, LANES), F32)
    edges = pltpu.VMEM((4, 4, RANGE, LANES), F32)
    dma = pltpu.SemaphoreType.DMA
    adjoint, gradient = pl.pallas_call(
        kernel,
        out_shape=(
            jax.ShapeDtypeStruct(density.shape, F32),
            jax.ShapeDtypeStruct((ROWS, LANES), F32),
        ),
        in_specs=[smem, hbm, hbm] + [vmem] * 11,
        out_specs=(vmem, vmem),
        scratch_shapes=[
            raw,
            raw,
            packed,
            packed,
            field,
            padded,
            pltpu.VMEM((MASS, RANGE, LANES), F32),
            pltpu.VMEM((BINS, LANES), F32),
            pltpu.VMEM((4, BINS, LANES), F32),
            matrix,
            matrix,
            matrix,
            matrix,
            small,
            small,
            padded,
            field,
            field,
            padded,
            field,
            field,
            padded,
            field,
            packed,
            edges,
            edges,
            small,
            pltpu.VMEM((3, 4, ROWS, LANES), F32),
            dma((2,)),
            dma((3, 3, ROWS)),
            dma((3, 3, ROWS)),
            dma((3,)),
            dma((3,)),
            dma((4, 4)),
            dma((4, 4)),
            dma((3, 3)),
            dma((3, 3)),
        ],
        compiler_params=pltpu.CompilerParams(
            collective_id=0, has_side_effects=True, vmem_limit_bytes=48 << 20
        ),
    )(
        frag_pairs,
        density,
        cotangent,
        drift_in,
        drift_out,
        spread[None, :],
        dest_bins[None, :],
        bott_split[None, :],
        coag_rate[None, :],
        frag_gain,
        frag_rate[None, :],
        collide_speed,
        frag_speed[None, :],
        regime,
    )
    return adjoint, gradient[0]


def solution(mesh):
    in_specs = (
        P("mass", "phi", "row"),
        P("mass", "phi", "row"),
        P("mass", None),
        P("mass", None),
        P("mass"),
        P(),
        P(),
        P(),
        P(),
        P(),
        P(),
        P("phi", "row"),
        P("row"),
        P("phi", "row"),
    )
    out_specs = (P("mass", "phi", "row"), P("row"))
    return jax.shard_map(
        per_device, mesh=mesh, in_specs=in_specs, out_specs=out_specs, check_vma=False
    )
```

```python
import functools

import jax
import jax.numpy as jnp
from jax import lax
from jax.experimental import pallas as pl
from jax.experimental.pallas import tpu as pltpu
from jax.sharding import PartitionSpec as P


MESH = pl.DeviceIdType.MESH
F32 = jnp.float32
BF16 = jnp.bfloat16
RANGE = 64
MASS = 4
ROWS = 8
BINS = 256
LANES = 128
GATE_WIDTH = 0.5
BACK, FORTH = 0, 1
EARLY = 2


def lanes_of(shape):
    return lax.broadcasted_iota(jnp.int32, shape, len(shape) - 1)


def rolled(value, shift):
    shift = shift % LANES
    return value if shift == 0 else pltpu.roll(value, shift, value.ndim - 1)


def swap_blocks(tiles):
    block = lanes_of(tiles[0].shape) // 32
    low = block < 2
    even = block % 2 == 0
    s0, s1, s2, s3 = tiles
    a0 = jnp.where(low, s0, rolled(s2, 64))
    a2 = jnp.where(low, rolled(s0, 64), s2)
    a1 = jnp.where(low, s1, rolled(s3, 64))
    a3 = jnp.where(low, rolled(s1, 64), s3)
    return (
        jnp.where(even, a0, rolled(a1, 32)),
        jnp.where(even, rolled(a0, 96), a1),
        jnp.where(even, a2, rolled(a3, 32)),
        jnp.where(even, rolled(a2, 96), a3),
    )


def high_low(value):
    high = value.astype(BF16)
    return high, (value - high.astype(F32)).astype(BF16)


def kernel(
    pairs_hbm,
    density,
    cotangent,
    drift_in,
    drift_out,
    spread_hbm,
    dest_hbm,
    split_hbm,
    rate_hbm,
    gain_hbm,
    frag_rate_hbm,
    speed_hbm,
    frag_speed_hbm,
    regime_hbm,
    out,
    grad,
    pairs,
    raw_c,
    raw_d,
    in_q,
    out_q,
    spread,
    dest,
    split,
    rate,
    gain,
    frag_rate,
    speed,
    frag_speed,
    regime,
    here,
    own_coef,
    there,
    pack_c,
    pack_d,
    cot,
    m1,
    coef_out,
    coef_in,
    coef,
    back,
    forth,
    gates,
    slopes,
    w2,
    f2,
    a1,
    w1,
    f1,
    st,
    res,
    ret,
    edge_out,
    edge_in,
    acc,
    red,
    load_sem,
    field_send,
    field_recv,
    coef_send,
    coef_recv,
    edge_send,
    edge_recv,
    red_send,
    red_recv,
):
    phi = lax.axis_index("phi")
    row = lax.axis_index("row")
    m = lax.axis_index("mass")
    phis = lax.axis_size("phi")
    rows = lax.axis_size("row")
    low = lax.rem(phi, 8)
    high = phi // 8
    corner = high * MASS + m

    at = pl.multiple_of(row * LANES, LANES)
    sources = (
        (cotangent, raw_c),
        (spread_hbm, spread),
        (drift_in.at[:, pl.ds(at, LANES)], in_q),
        (drift_out.at[:, pl.ds(at, LANES)], out_q),
        (density, raw_d),
        (dest_hbm, dest),
        (split_hbm, split),
        (rate_hbm, rate),
        (gain_hbm, gain),
        (frag_rate_hbm, frag_rate),
        (pairs_hbm, pairs),
        (speed_hbm, speed),
        (frag_speed_hbm, frag_speed),
        (regime_hbm, regime),
    )
    loads = [pltpu.make_async_copy(x, y, load_sem.at[i]) for i, (x, y) in enumerate(sources)]
    for load in loads:
        load.start()

    def mass_peer(k):
        return {"mass": lax.rem(m + k, MASS)}

    def low_peer(k):
        return {"phi": high * 8 + lax.rem(low + k, 8)}

    def corner_peer(k):
        other = lax.rem(corner + k, 8)
        return {"phi": (other // MASS) * 8 + low, "mass": lax.rem(other, MASS)}

    radial = row * MASS + m
    radials = rows * MASS
    right_at = lax.rem(radial + 1, radials)
    left_at = lax.rem(radial + radials - 1, radials)
    right = {"row": right_at // MASS, "mass": lax.rem(right_at, MASS)}
    left = {"row": left_at // MASS, "mass": lax.rem(left_at, MASS)}
    row_right = {"row": lax.rem(row + 1, rows)}
    row_left = {"row": lax.rem(row + rows - 1, rows)}
    after = {"phi": lax.rem(phi + 1, phis)}
    before = {"phi": lax.rem(phi + phis - 1, phis)}

    barrier = pltpu.get_barrier_semaphore()
    greeted = [mass_peer(k) for k in (1, 2, 3)]
    greeted += [right, left, row_right, row_left, after, before]
    greeted += [low_peer(k) for k in range(1, 8)] + [corner_peer(k) for k in range(1, 8)]
    for device in greeted:
        pl.semaphore_signal(barrier, inc=1, device_id=device, device_id_type=MESH)

    tile = (RANGE, LANES)
    lane = lanes_of(tile)
    block = lane // 32
    within = lax.rem(lane, 32)
    first = within == 0
    final = within == 31
    zero = jnp.zeros(tile, F32)

    def field_copy(kind, k, ah, source, target):
        return pltpu.make_async_remote_copy(
            src_ref=source,
            dst_ref=target,
            send_sem=field_send.at[kind, k - 1, ah],
            recv_sem=field_recv.at[kind, k - 1, ah],
            device_id=mass_peer(k),
            device_id_type=MESH,
        )

    own = pl.ds(pl.multiple_of(m * RANGE, RANGE), RANGE)

    def cot_copy(k, ah):
        return field_copy(0, k, ah, pack_c.at[lax.rem(m + k, MASS), ah], cot.at[ah, own])

    def m1_copy(k, ah):
        return field_copy(1, k, ah, pack_d.at[lax.rem(m + k, MASS), ah], m1.at[ah, own])

    def ret_copy(k, ah):
        theirs = pl.ds(pl.multiple_of(lax.rem(m + k, MASS) * RANGE, RANGE), RANGE)
        return field_copy(2, k, ah, res.at[ah, theirs], ret.at[m, ah])

    def coef_copy(k):
        return pltpu.make_async_remote_copy(
            src_ref=coef_out.at[lax.rem(m + k, MASS)],
            dst_ref=coef_in.at[own],
            send_sem=coef_send.at[k - 1],
            recv_sem=coef_recv.at[k - 1],
            device_id=mass_peer(k),
            device_id_type=MESH,
        )

    def edge_copy(n, i):
        device = ((row_right, row_left) if n == 2 else (right, left)) + (after, before)
        return pltpu.make_async_remote_copy(
            src_ref=edge_out.at[n, i],
            dst_ref=edge_in.at[n, i],
            send_sem=edge_send.at[n, i],
            recv_sem=edge_recv.at[n, i],
            device_id=device[i],
            device_id_type=MESH,
        )

    flat_c = raw_c.reshape(RANGE * 32, LANES)

    def send_cot(i, carry):
        ah = lax.rem(i + 7, 8)
        tiles = swap_blocks([flat_c[pl.ds(al * 8 + ah, RANGE, stride=32), :] for al in range(4)])
        for k in range(MASS):
            pack_c[k, ah] = tiles[k]
        for k in (1, 2, 3):
            cot_copy(k, ah).start()
        cot[ah, own] = pack_c[m, ah]
        return carry

    loads[0].wait()
    pl.semaphore_wait(barrier, len(greeted))
    lax.fori_loop(0, ROWS, send_cot, 0)

    for i in (1, 2, 3):
        loads[i].wait()
    square = (RANGE, RANGE)
    on_diag = lax.broadcasted_iota(jnp.int32, square, 0) == lanes_of(square)
    spread_col = jnp.sum(jnp.where(on_diag, jnp.broadcast_to(spread[...], square), 0.0), axis=1, keepdims=True)
    spread_tile = jnp.broadcast_to(spread_col, tile)
    for k in range(MASS):
        coef_out[k] = jnp.where(
            block == 0,
            rolled(in_q[...], -32 * k),
            jnp.where(block == 1, rolled(out_q[...], 32 - 32 * k), spread_tile),
        )
    for k in (1, 2, 3):
        coef_copy(k).start()
    coef_in[own] = coef_out[m]
    own_coef[0] = 1.0 - in_q[...] - out_q[...] - 2.0 * spread_tile
    own_coef[1] = spread_tile

    loads[4].wait()
    flat_d = raw_d.reshape(RANGE * 32, LANES)
    edge_out[2, 2] = flat_d[pl.ds(31, RANGE, stride=32), :]
    edge_out[2, 3] = flat_d[pl.ds(0, RANGE, stride=32), :]
    edge_copy(2, 2).start()
    edge_copy(2, 3).start()
    lowest = lane == 0
    topmost = lane == LANES - 1

    def own_edges(i, carry):
        last_col, first_col = carry
        for k in range(4):
            a = i * 4 + k
            value = flat_d[pl.ds(a, RANGE, stride=32), :]
            here[a + 1] = value
            last_col = jnp.where(topmost, out_q[...] * value, rolled(last_col, -1))
            first_col = jnp.where(lowest, in_q[...] * value, rolled(first_col, 1))
        return last_col, first_col

    last_col, first_col = lax.fori_loop(0, 8, own_edges, (zero, zero))
    edge_out[2, 0] = last_col
    edge_out[2, 1] = first_col
    edge_copy(2, 0).start()
    edge_copy(2, 1).start()

    for load in loads[5:]:
        load.wait()
    whole = (BINS, BINS)
    row_ids = lax.broadcasted_iota(jnp.int32, whole, 0)
    col_ids = lanes_of(whole)
    target = jnp.broadcast_to(dest[...], whole)
    upper = jnp.broadcast_to(split[...], whole)
    diag = jnp.where(row_ids == col_ids, 1.0, 0.0)
    coag_full = (
        jnp.where(row_ids == target, 1.0 - upper, 0.0) + jnp.where(row_ids == target + 1, upper, 0.0) - diag
    ) * rate[...]
    strip = (RANGE, BINS)
    strip_block = lanes_of(strip) // RANGE
    chosen = []
    for i in range(MASS):
        line = jnp.zeros(strip, F32)
        for j in range(MASS):
            line = jnp.where(strip_block == j, pairs[i, j].astype(F32), line)
        chosen.append(line)
    chosen = jnp.concatenate(chosen, axis=0)
    frag_full = gain[...] * chosen * jnp.where(row_ids <= col_ids, 1.0, 0.0) - diag * frag_rate[...]
    for at_row, matrix in ((0, coag_full), (BINS, frag_full)):
        for kept, value in ((forth, matrix), (back, matrix.T)):
            hi, lo = high_low(value)
            kept[at_row : at_row + BINS, 0:BINS] = hi
            kept[at_row : at_row + BINS, BINS : 2 * BINS] = hi
            kept[at_row : at_row + BINS, 2 * BINS : 3 * BINS] = lo

    sigma = 1.0 / (1.0 + jnp.exp(-((speed[...] - frag_speed[...]) / GATE_WIDTH)))
    flagged = regime[...].astype(F32)
    gate_all = flagged * sigma
    slope_all = -flagged * sigma * (1.0 - sigma) / GATE_WIDTH
    block8 = lanes_of((ROWS, LANES)) // 32
    for source, kept in ((gate_all, gates), (slope_all, slopes)):
        value = jnp.zeros((ROWS, LANES), F32)
        for al in range(4):
            part = pltpu.roll(source[al * 8 : al * 8 + 8], lax.rem(32 * (al + MASS - m), LANES), 1)
            value = jnp.where(block8 == al, part, value)
        kept[...] = value

    for i in range(4):
        edge_copy(2, i).wait_recv()
    here[0] = edge_in[2, 2]
    here[33] = edge_in[2, 3]
    row_has_left = jnp.where(row > 0, 1.0, 0.0)
    row_has_right = jnp.where(row < rows - 1, 1.0, 0.0)

    def own_forward(i, carry):
        last_col, first_col = carry
        for k in range(4):
            a = i * 4 + k
            value = here[a + 1]
            beside = here[a] + here[a + 2]
            outer = jnp.where(topmost, first_col, rolled(in_q[...] * value, -1))
            inner = jnp.where(lowest, last_col, rolled(out_q[...] * value, 1))
            there[a] = own_coef[0] * value + outer + inner + own_coef[1] * beside
            last_col = rolled(last_col, -1)
            first_col = rolled(first_col, 1)
        return last_col, first_col

    lax.fori_loop(
        0,
        8,
        own_forward,
        (rolled(edge_in[2, 0], 32) * row_has_left, rolled(edge_in[2, 1], 96) * row_has_right),
    )

    def pack_m1(ah, carry):
        tiles = swap_blocks([there[al * 8 + ah] for al in range(4)])
        for k in range(MASS):
            pack_d[k, ah] = tiles[k]
        m1[ah, own] = pack_d[m, ah]
        return carry

    lax.fori_loop(0, ROWS, pack_m1, 0)

    def send_m1(i, carry):
        for k in (1, 2, 3):
            m1_copy(k, lax.rem(i + 7, 8)).start()
        return carry

    lax.fori_loop(0, EARLY, send_m1, 0)

    has_left = jnp.where(radial > 0, 1.0, 0.0)
    has_right = jnp.where(radial < radials - 1, 1.0, 0.0)

    def mix(n, source, matrix, way, state, arrive, seen):
        edge_out[n, 0] = zero
        edge_out[n, 1] = zero

        def body(j, carry):
            pair = (lax.rem(2 * j + 7, 8), 2 * j)
            for ah in pair:
                arrive(ah)
            x = jnp.concatenate([source[ah] for ah in pair], axis=1)
            x_hi, x_lo = high_low(x)
            y = jnp.dot(matrix[...], jnp.concatenate([x_hi, x_lo, x_hi], axis=0), preferred_element_type=F32)
            gate = jnp.concatenate([gates[pl.ds(ah, 1)] for ah in pair], axis=1)
            new = x + (y[:BINS] + gate * y[BINS:])
            for half, ah in enumerate(pair):
                lanes = slice(half * LANES, (half + 1) * LANES)
                state[ah + 1] = new[:, lanes]
                seen(ah, x[:, lanes], y[BINS:, lanes])
                last_col, first_col = edge_out[n, 0], edge_out[n, 1]
                for g in range(MASS):
                    bins = slice(g * RANGE, (g + 1) * RANGE)
                    value = new[bins, lanes]
                    to_left = value * coef[0, bins] if way == FORTH else value
                    to_right = value * coef[1, bins] if way == FORTH else value
                    last_col = jnp.where(final, to_right, rolled(last_col, -1))
                    first_col = jnp.where(first, to_left, rolled(first_col, 1))
                edge_out[n, 0] = last_col
                edge_out[n, 1] = first_col

            @pl.when(j == 0)
            def _():
                for i, ah in ((2, ROWS), (3, 1)):
                    value = zero
                    for g in range(MASS):
                        bins = slice(g * RANGE, (g + 1) * RANGE)
                        part = rolled(state[ah, bins], 32 * (g - 3) if i == 2 else 32 * g)
                        value = jnp.where(block == g, part, value)
                    edge_out[n, i] = value
                    edge_copy(n, i).start()

            return carry

        lax.fori_loop(0, ROWS // 2, body, 0)
        edge_copy(n, 0).start()
        edge_copy(n, 1).start()

    def stencil(n, field, way, emit, after_row=None):
        edge_copy(n, 0).wait_recv()
        edge_copy(n, 1).wait_recv()

        def body(i, carry):
            last_col, first_col = carry
            ah = lax.rem(14 - i, 8)
            for g in reversed(range(MASS)):
                bins = slice(g * RANGE, (g + 1) * RANGE)
                value = field[ah + 1, bins]
                beside = field[ah, bins] + field[ah + 2, bins]
                c_in, c_out = coef[0, bins], coef[1, bins]
                to_left = c_in * value if way == FORTH else value
                to_right = c_out * value if way == FORTH else value
                outer = rolled(jnp.where(first, first_col, to_left), -1)
                inner = rolled(jnp.where(final, last_col, to_right), 1)
                both = outer + inner if way == FORTH else c_in * inner + c_out * outer
                emit(ah, bins, coef[3, bins] * value + both + coef[2, bins] * beside)
                last_col = rolled(last_col, 1)
                first_col = rolled(first_col, -1)
            if after_row is not None:
                after_row(ah)
            return last_col, first_col

        carry = (rolled(edge_in[n, 0], -32) * has_left, rolled(edge_in[n, 1], 32) * has_right)
        carry = lax.fori_loop(0, 6, body, carry)
        edge_copy(n, 2).wait_recv()
        edge_copy(n, 3).wait_recv()
        for g in range(MASS):
            bins = slice(g * RANGE, (g + 1) * RANGE)
            field[0, bins] = jnp.where(
                block == 0, rolled(edge_in[n, 2], -32 * g), rolled(field[ROWS, bins], 32)
            )
            field[ROWS + 1, bins] = jnp.where(
                block == 3, rolled(edge_in[n, 3], 32 * (3 - g)), rolled(field[1, bins], -32)
            )
        lax.fori_loop(6, 8, body, carry)

    def add_product(ah, value, other):
        summed = jnp.sum((value * other).reshape(-1, 8, LANES), axis=0)
        acc[...] += slopes[pl.ds(ah, 1)] * summed

    def arrived(copy):
        def wait(ah):
            for k in (1, 2, 3):
                copy(k, ah).wait_recv()

        return wait

    acc[...] = jnp.zeros((8, LANES), F32)

    def keep_f2(ah, x, frags):
        f2[ah] = frags

    mix(0, cot, back, BACK, w2, arrived(cot_copy), keep_f2)
    lax.fori_loop(EARLY, ROWS, send_m1, 0)

    for k in (1, 2, 3):
        coef_copy(k).wait_recv()
    for g in range(MASS):
        bins = slice(g * RANGE, (g + 1) * RANGE)
        turns = [rolled(coef_in[bins], 32 * k) for k in range(4)]

        def everywhere(source):
            value = turns[(0 - source) % 4]
            for b in (1, 2, 3):
                value = jnp.where(block == b, turns[(b - source) % 4], value)
            return value

        c_in, c_out, c_spread = everywhere(0), everywhere(1), everywhere(2)
        coef[0, bins] = c_in
        coef[1, bins] = c_out
        coef[2, bins] = c_spread
        coef[3, bins] = 1.0 - c_in - c_out - 2.0 * c_spread

    def keep_a1(ah, bins, value):
        a1[ah, bins] = value

    stencil(0, w2, BACK, keep_a1)

    def keep_f1(ah, x, frags):
        f1[ah] = frags

    mix(1, a1, back, BACK, w1, lambda ah: None, keep_f1)

    def first_product(ah, x, frags):
        add_product(ah, x, f1[ah])

    mix(3, m1, forth, FORTH, st, arrived(m1_copy), first_product)

    def keep_res(ah, bins, value):
        res[ah, bins] = value

    def send_row(ah):
        for k in (1, 2, 3):
            ret_copy(k, ah).start()
        ret[m, ah] = res[ah, own]

    stencil(1, w1, BACK, keep_res, send_row)

    def second_product(ah, bins, value):
        add_product(ah, value, f2[ah, bins])

    stencil(3, st, FORTH, second_product)

    flat_out = out.reshape(RANGE * 32, LANES)

    def unpack(i, carry):
        ah = lax.rem(14 - i, 8)
        arrived(ret_copy)(ah)
        tiles = swap_blocks([ret[k, ah] for k in range(MASS)])
        for al in range(4):
            flat_out[pl.ds(al * 8 + ah, RANGE, stride=32), :] = tiles[al]
        return carry

    total = jnp.sum(acc[...], axis=0, keepdims=True)
    total = total + rolled(total, 32) + rolled(total, 64) + rolled(total, 96)
    total = jnp.broadcast_to(total, (8, LANES))
    total = jnp.where(block8 == m, total, 0.0)
    for n, (place, peer) in enumerate(((low, low_peer), (corner, corner_peer))):
        red[n, place] = total
        copies = []
        for k in range(1, 8):
            copies.append(
                pltpu.make_async_remote_copy(
                    src_ref=red.at[n, place],
                    dst_ref=red.at[n, place],
                    send_sem=red_send.at[n, k - 1],
                    recv_sem=red_recv.at[n, k - 1],
                    device_id=peer(k),
                    device_id_type=MESH,
                )
            )
        for copy in copies:
            copy.start()
        lax.fori_loop(4 * n, 4 * n + 4, unpack, 0)
        for copy in copies:
            copy.wait()
        total = ((red[n, 0] + red[n, 1]) + (red[n, 2] + red[n, 3])) + (
            (red[n, 4] + red[n, 5]) + (red[n, 6] + red[n, 7])
        )
    grad[...] = total[0:1]

    def drain(ah, carry):
        for copy in (cot_copy, m1_copy, ret_copy):
            for k in (1, 2, 3):
                copy(k, ah).wait_send()
        return carry

    lax.fori_loop(0, ROWS, drain, 0)
    for k in (1, 2, 3):
        coef_copy(k).wait_send()
    for n in range(4):
        for i in range(4):
            edge_copy(n, i).wait_send()


def per_device(
    density,
    cotangent,
    drift_in,
    drift_out,
    spread,
    dest_bins,
    bott_split,
    coag_rate,
    frag_pairs,
    frag_gain,
    frag_rate,
    collide_speed,
    frag_speed,
    regime,
):
    vmem = pl.BlockSpec(memory_space=pltpu.VMEM)
    hbm = pl.BlockSpec(memory_space=pltpu.HBM)
    field = pltpu.VMEM((ROWS, BINS, LANES), F32)
    padded = pltpu.VMEM((ROWS + 2, BINS, LANES), F32)
    packed = pltpu.VMEM((MASS, ROWS, RANGE, LANES), F32)
    raw = pltpu.VMEM(density.shape, F32)
    matrix = pltpu.VMEM((2 * BINS, 3 * BINS), BF16)
    small = pltpu.VMEM((ROWS, LANES), F32)
    edges = pltpu.VMEM((4, 4, RANGE, LANES), F32)
    tile = pltpu.VMEM((RANGE, LANES), F32)
    per_bin = pltpu.VMEM((1, BINS), F32)
    cells = pltpu.VMEM((32, LANES), F32)
    dma = pltpu.SemaphoreType.DMA
    adjoint, gradient = pl.pallas_call(
        kernel,
        out_shape=(
            jax.ShapeDtypeStruct(density.shape, F32),
            jax.ShapeDtypeStruct((1, LANES), F32),
        ),
        in_specs=[hbm] * 14,
        out_specs=(vmem, vmem),
        scratch_shapes=[
            pltpu.SMEM((MASS, MASS), jnp.int32),
            raw,
            raw,
            tile,
            tile,
            pltpu.VMEM((1, RANGE), F32),
            pltpu.VMEM((1, BINS), jnp.int32),
            per_bin,
            per_bin,
            pltpu.VMEM((BINS, BINS), F32),
            per_bin,
            cells,
            pltpu.VMEM((1, LANES), F32),
            pltpu.VMEM((32, LANES), jnp.int32),
            pltpu.VMEM((34, RANGE, LANES), F32),
            pltpu.VMEM((2, RANGE, LANES), F32),
            pltpu.VMEM((32, RANGE, LANES), F32),
            packed,
            packed,
            field,
            field,
            pltpu.VMEM((MASS, RANGE, LANES), F32),
            pltpu.VMEM((BINS, LANES), F32),
            pltpu.VMEM((4, BINS, LANES), F32),
            matrix,
            matrix,
            small,
            small,
            padded,
            field,
            field,
            padded,
            field,
            padded,
            field,
            packed,
            edges,
            edges,
            small,
            pltpu.VMEM((2, 8, ROWS, LANES), F32),
            dma((14,)),
            dma((3, 3, ROWS)),
            dma((3, 3, ROWS)),
            dma((3,)),
            dma((3,)),
            dma((4, 4)),
            dma((4, 4)),
            dma((2, 7)),
            dma((2, 7)),
        ],
        compiler_params=pltpu.CompilerParams(
            collective_id=0, has_side_effects=True, vmem_limit_bytes=48 << 20
        ),
    )(
        frag_pairs,
        density,
        cotangent,
        drift_in,
        drift_out,
        spread[None, :],
        dest_bins[None, :],
        bott_split[None, :],
        coag_rate[None, :],
        frag_gain,
        frag_rate[None, :],
        collide_speed,
        frag_speed[None, :],
        regime,
    )
    return adjoint, gradient[0]


def solution(mesh):
    in_specs = (
        P("mass", "phi", "row"),
        P("mass", "phi", "row"),
        P("mass", None),
        P("mass", None),
        P("mass"),
        P(),
        P(),
        P(),
        P(),
        P(),
        P(),
        P("phi", "row"),
        P("row"),
        P("phi", "row"),
    )
    out_specs = (P("mass", "phi", "row"), P("row"))
    return jax.shard_map(
        per_device, mesh=mesh, in_specs=in_specs, out_specs=out_specs, check_vma=False
    )
```

```python
import functools

import jax
import jax.numpy as jnp
from jax import lax
from jax.experimental import pallas as pl
from jax.experimental.pallas import tpu as pltpu
from jax.sharding import PartitionSpec as P


MESH = pl.DeviceIdType.MESH
F32 = jnp.float32
BF16 = jnp.bfloat16
RANGE = 64
MASS = 4
ROWS = 8
BINS = 256
LANES = 128
GATE_WIDTH = 0.5
BACK, FORTH = 0, 1
EARLY = 2


def lanes_of(shape):
    return lax.broadcasted_iota(jnp.int32, shape, len(shape) - 1)


def rolled(value, shift):
    shift = shift % LANES
    return value if shift == 0 else pltpu.roll(value, shift, value.ndim - 1)


def swap_blocks(tiles):
    block = lanes_of(tiles[0].shape) // 32
    low = block < 2
    even = block % 2 == 0
    s0, s1, s2, s3 = tiles
    a0 = jnp.where(low, s0, rolled(s2, 64))
    a2 = jnp.where(low, rolled(s0, 64), s2)
    a1 = jnp.where(low, s1, rolled(s3, 64))
    a3 = jnp.where(low, rolled(s1, 64), s3)
    return (
        jnp.where(even, a0, rolled(a1, 32)),
        jnp.where(even, rolled(a0, 96), a1),
        jnp.where(even, a2, rolled(a3, 32)),
        jnp.where(even, rolled(a2, 96), a3),
    )


def high_low(value):
    high = value.astype(BF16)
    return high, (value - high.astype(F32)).astype(BF16)


def kernel(
    pairs_hbm,
    density,
    cotangent,
    drift_in,
    drift_out,
    spread_hbm,
    dest_hbm,
    split_hbm,
    rate_hbm,
    gain_hbm,
    frag_rate_hbm,
    speed_hbm,
    frag_speed_hbm,
    regime_hbm,
    out,
    grad,
    pairs,
    raw_c,
    raw_d,
    in_q,
    out_q,
    spread,
    dest,
    split,
    rate,
    gain,
    frag_rate,
    speed,
    frag_speed,
    regime,
    here,
    own_coef,
    there,
    pack_c,
    pack_d,
    cot,
    m1,
    coef_out,
    coef_in,
    coef,
    back,
    forth,
    gates,
    slopes,
    w2,
    f2,
    a1,
    w1,
    f1,
    st,
    res,
    ret,
    edge_out,
    edge_in,
    acc,
    red,
    load_sem,
    field_send,
    field_recv,
    coef_send,
    coef_recv,
    edge_send,
    edge_recv,
    red_send,
    red_recv,
):
    phi = lax.axis_index("phi")
    row = lax.axis_index("row")
    m = lax.axis_index("mass")
    phis = lax.axis_size("phi")
    rows = lax.axis_size("row")
    low = lax.rem(phi, 8)
    high = phi // 8
    corner = high * MASS + m

    at = pl.multiple_of(row * LANES, LANES)
    sources = (
        (cotangent, raw_c),
        (spread_hbm, spread),
        (drift_in.at[:, pl.ds(at, LANES)], in_q),
        (drift_out.at[:, pl.ds(at, LANES)], out_q),
        (density, raw_d),
        (dest_hbm, dest),
        (split_hbm, split),
        (rate_hbm, rate),
        (gain_hbm, gain),
        (frag_rate_hbm, frag_rate),
        (pairs_hbm, pairs),
        (speed_hbm, speed),
        (frag_speed_hbm, frag_speed),
        (regime_hbm, regime),
    )
    loads = [pltpu.make_async_copy(x, y, load_sem.at[i]) for i, (x, y) in enumerate(sources)]
    for load in loads:
        load.start()

    def mass_peer(k):
        return {"mass": lax.rem(m + k, MASS)}

    def low_peer(k):
        return {"phi": high * 8 + lax.rem(low + k, 8)}

    def corner_peer(k):
        other = lax.rem(corner + k, 8)
        return {"phi": (other // MASS) * 8 + low, "mass": lax.rem(other, MASS)}

    radial = row * MASS + m
    radials = rows * MASS
    right_at = lax.rem(radial + 1, radials)
    left_at = lax.rem(radial + radials - 1, radials)
    right = {"row": right_at // MASS, "mass": lax.rem(right_at, MASS)}
    left = {"row": left_at // MASS, "mass": lax.rem(left_at, MASS)}
    row_right = {"row": lax.rem(row + 1, rows)}
    row_left = {"row": lax.rem(row + rows - 1, rows)}
    after = {"phi": lax.rem(phi + 1, phis)}
    before = {"phi": lax.rem(phi + phis - 1, phis)}

    barrier = pltpu.get_barrier_semaphore()
    greeted = [mass_peer(k) for k in (1, 2, 3)]
    greeted += [right, left, row_right, row_left, after, before]
    greeted += [low_peer(k) for k in range(1, 8)] + [corner_peer(k) for k in range(1, 8)]
    for device in greeted:
        pl.semaphore_signal(barrier, inc=1, device_id=device, device_id_type=MESH)

    tile = (RANGE, LANES)
    lane = lanes_of(tile)
    block = lane // 32
    within = lax.rem(lane, 32)
    first = within == 0
    final = within == 31
    zero = jnp.zeros(tile, F32)

    def field_copy(kind, k, ah, source, target):
        return pltpu.make_async_remote_copy(
            src_ref=source,
            dst_ref=target,
            send_sem=field_send.at[kind, k - 1, ah],
            recv_sem=field_recv.at[kind, k - 1, ah],
            device_id=mass_peer(k),
            device_id_type=MESH,
        )

    own = pl.ds(pl.multiple_of(m * RANGE, RANGE), RANGE)

    def cot_copy(k, ah):
        return field_copy(0, k, ah, pack_c.at[lax.rem(m + k, MASS), ah], cot.at[ah, own])

    def m1_copy(k, ah):
        return field_copy(1, k, ah, pack_d.at[lax.rem(m + k, MASS), ah], m1.at[ah, own])

    def ret_copy(k, ah):
        theirs = pl.ds(pl.multiple_of(lax.rem(m + k, MASS) * RANGE, RANGE), RANGE)
        return field_copy(2, k, ah, res.at[ah, theirs], ret.at[m, ah])

    def coef_copy(k):
        return pltpu.make_async_remote_copy(
            src_ref=coef_out.at[lax.rem(m + k, MASS)],
            dst_ref=coef_in.at[own],
            send_sem=coef_send.at[k - 1],
            recv_sem=coef_recv.at[k - 1],
            device_id=mass_peer(k),
            device_id_type=MESH,
        )

    def edge_copy(n, i):
        device = ((row_right, row_left) if n == 2 else (right, left)) + (after, before)
        return pltpu.make_async_remote_copy(
            src_ref=edge_out.at[n, i],
            dst_ref=edge_in.at[n, i],
            send_sem=edge_send.at[n, i],
            recv_sem=edge_recv.at[n, i],
            device_id=device[i],
            device_id_type=MESH,
        )

    flat_c = raw_c.reshape(RANGE * 32, LANES)

    def send_cot(i, carry):
        ah = lax.rem(i + 7, 8)
        tiles = swap_blocks([flat_c[pl.ds(al * 8 + ah, RANGE, stride=32), :] for al in range(4)])
        for k in range(MASS):
            pack_c[k, ah] = tiles[k]
        for k in (1, 2, 3):
            cot_copy(k, ah).start()
        cot[ah, own] = pack_c[m, ah]
        return carry

    loads[0].wait()
    pl.semaphore_wait(barrier, len(greeted))
    lax.fori_loop(0, ROWS, send_cot, 0)

    for i in (1, 2, 3):
        loads[i].wait()
    square = (RANGE, RANGE)
    on_diag = lax.broadcasted_iota(jnp.int32, square, 0) == lanes_of(square)
    spread_col = jnp.sum(jnp.where(on_diag, jnp.broadcast_to(spread[...], square), 0.0), axis=1, keepdims=True)
    spread_tile = jnp.broadcast_to(spread_col, tile)
    for k in range(MASS):
        coef_out[k] = jnp.where(
            block == 0,
            rolled(in_q[...], -32 * k),
            jnp.where(block == 1, rolled(out_q[...], 32 - 32 * k), spread_tile),
        )
    for k in (1, 2, 3):
        coef_copy(k).start()
    coef_in[own] = coef_out[m]
    own_coef[0] = 1.0 - in_q[...] - out_q[...] - 2.0 * spread_tile
    own_coef[1] = spread_tile

    loads[4].wait()
    flat_d = raw_d.reshape(RANGE * 32, LANES)
    edge_out[2, 2] = flat_d[pl.ds(31, RANGE, stride=32), :]
    edge_out[2, 3] = flat_d[pl.ds(0, RANGE, stride=32), :]
    edge_copy(2, 2).start()
    edge_copy(2, 3).start()
    lowest = lane == 0
    topmost = lane == LANES - 1

    def own_edges(i, carry):
        last_col, first_col = carry
        for k in range(4):
            a = i * 4 + k
            value = flat_d[pl.ds(a, RANGE, stride=32), :]
            here[a + 1] = value
            last_col = jnp.where(topmost, out_q[...] * value, rolled(last_col, -1))
            first_col = jnp.where(lowest, in_q[...] * value, rolled(first_col, 1))
        return last_col, first_col

    last_col, first_col = lax.fori_loop(0, 8, own_edges, (zero, zero))
    edge_out[2, 0] = last_col
    edge_out[2, 1] = first_col
    edge_copy(2, 0).start()
    edge_copy(2, 1).start()

    for load in loads[5:]:
        load.wait()
    whole = (BINS, BINS)
    row_ids = lax.broadcasted_iota(jnp.int32, whole, 0)
    col_ids = lanes_of(whole)
    target = jnp.broadcast_to(dest[...], whole)
    upper = jnp.broadcast_to(split[...], whole)
    diag = jnp.where(row_ids == col_ids, 1.0, 0.0)
    coag_full = (
        jnp.where(row_ids == target, 1.0 - upper, 0.0) + jnp.where(row_ids == target + 1, upper, 0.0) - diag
    ) * rate[...]
    strip = (RANGE, BINS)
    strip_block = lanes_of(strip) // RANGE
    chosen = []
    for i in range(MASS):
        line = jnp.zeros(strip, F32)
        for j in range(MASS):
            line = jnp.where(strip_block == j, pairs[i, j].astype(F32), line)
        chosen.append(line)
    chosen = jnp.concatenate(chosen, axis=0)
    frag_full = gain[...] * chosen * jnp.where(row_ids <= col_ids, 1.0, 0.0) - diag * frag_rate[...]
    for at_row, matrix in ((0, coag_full), (BINS, frag_full)):
        for kept, value in ((forth, matrix), (back, matrix.T)):
            hi, lo = high_low(value)
            kept[at_row : at_row + BINS, 0:BINS] = hi
            kept[at_row : at_row + BINS, BINS : 2 * BINS] = hi
            kept[at_row : at_row + BINS, 2 * BINS : 3 * BINS] = lo

    sigma = 1.0 / (1.0 + jnp.exp(-((speed[...] - frag_speed[...]) / GATE_WIDTH)))
    flagged = regime[...].astype(F32)
    gate_all = flagged * sigma
    slope_all = -flagged * sigma * (1.0 - sigma) / GATE_WIDTH
    block8 = lanes_of((ROWS, LANES)) // 32
    for source, kept in ((gate_all, gates), (slope_all, slopes)):
        value = jnp.zeros((ROWS, LANES), F32)
        for al in range(4):
            part = pltpu.roll(source[al * 8 : al * 8 + 8], lax.rem(32 * (al + MASS - m), LANES), 1)
            value = jnp.where(block8 == al, part, value)
        kept[...] = value

    for i in range(4):
        edge_copy(2, i).wait_recv()
    here[0] = edge_in[2, 2]
    here[33] = edge_in[2, 3]
    row_has_left = jnp.where(row > 0, 1.0, 0.0)
    row_has_right = jnp.where(row < rows - 1, 1.0, 0.0)

    def own_forward(i, carry):
        last_col, first_col = carry
        for k in range(4):
            a = i * 4 + k
            value = here[a + 1]
            beside = here[a] + here[a + 2]
            outer = jnp.where(topmost, first_col, rolled(in_q[...] * value, -1))
            inner = jnp.where(lowest, last_col, rolled(out_q[...] * value, 1))
            there[a] = own_coef[0] * value + outer + inner + own_coef[1] * beside
            last_col = rolled(last_col, -1)
            first_col = rolled(first_col, 1)
        return last_col, first_col

    lax.fori_loop(
        0,
        8,
        own_forward,
        (rolled(edge_in[2, 0], 32) * row_has_left, rolled(edge_in[2, 1], 96) * row_has_right),
    )

    def pack_m1(ah, carry):
        tiles = swap_blocks([there[al * 8 + ah] for al in range(4)])
        for k in range(MASS):
            pack_d[k, ah] = tiles[k]
        m1[ah, own] = pack_d[m, ah]
        return carry

    lax.fori_loop(0, ROWS, pack_m1, 0)

    def send_m1(i, carry):
        for k in (1, 2, 3):
            m1_copy(k, lax.rem(i + 7, 8)).start()
        return carry

    lax.fori_loop(0, EARLY, send_m1, 0)

    has_left = jnp.where(radial > 0, 1.0, 0.0)
    has_right = jnp.where(radial < radials - 1, 1.0, 0.0)

    def mix(n, source, matrix, way, state, arrive, seen):
        edge_out[n, 0] = zero
        edge_out[n, 1] = zero

        def body(j, carry):
            pair = (lax.rem(2 * j + 7, 8), 2 * j)
            for ah in pair:
                arrive(ah)
            x = jnp.concatenate([source[ah] for ah in pair], axis=1)
            x_hi, x_lo = high_low(x)
            y = jnp.dot(matrix[...], jnp.concatenate([x_hi, x_lo, x_hi], axis=0), preferred_element_type=F32)
            gate = jnp.concatenate([gates[pl.ds(ah, 1)] for ah in pair], axis=1)
            new = x + (y[:BINS] + gate * y[BINS:])
            for half, ah in enumerate(pair):
                lanes = slice(half * LANES, (half + 1) * LANES)
                state[ah + 1] = new[:, lanes]
                seen(ah, x[:, lanes], y[BINS:, lanes])
                last_col, first_col = edge_out[n, 0], edge_out[n, 1]
                for g in range(MASS):
                    bins = slice(g * RANGE, (g + 1) * RANGE)
                    value = new[bins, lanes]
                    to_left = value * coef[0, bins] if way == FORTH else value
                    to_right = value * coef[1, bins] if way == FORTH else value
                    last_col = jnp.where(final, to_right, rolled(last_col, -1))
                    first_col = jnp.where(first, to_left, rolled(first_col, 1))
                edge_out[n, 0] = last_col
                edge_out[n, 1] = first_col

            @pl.when(j == 0)
            def _():
                for i, ah in ((2, ROWS), (3, 1)):
                    value = zero
                    for g in range(MASS):
                        bins = slice(g * RANGE, (g + 1) * RANGE)
                        part = rolled(state[ah, bins], 32 * (g - 3) if i == 2 else 32 * g)
                        value = jnp.where(block == g, part, value)
                    edge_out[n, i] = value
                    edge_copy(n, i).start()

            return carry

        lax.fori_loop(0, ROWS // 2, body, 0)
        edge_copy(n, 0).start()
        edge_copy(n, 1).start()

    def stencil(n, field, way, emit, after_row=None):
        edge_copy(n, 0).wait_recv()
        edge_copy(n, 1).wait_recv()

        def body(i, carry):
            last_col, first_col = carry
            ah = lax.rem(14 - i, 8)
            for g in reversed(range(MASS)):
                bins = slice(g * RANGE, (g + 1) * RANGE)
                value = field[ah + 1, bins]
                beside = field[ah, bins] + field[ah + 2, bins]
                c_in, c_out = coef[0, bins], coef[1, bins]
                to_left = c_in * value if way == FORTH else value
                to_right = c_out * value if way == FORTH else value
                outer = rolled(jnp.where(first, first_col, to_left), -1)
                inner = rolled(jnp.where(final, last_col, to_right), 1)
                both = outer + inner if way == FORTH else c_in * inner + c_out * outer
                emit(ah, bins, coef[3, bins] * value + both + coef[2, bins] * beside)
                last_col = rolled(last_col, 1)
                first_col = rolled(first_col, -1)
            if after_row is not None:
                after_row(ah)
            return last_col, first_col

        carry = (rolled(edge_in[n, 0], -32) * has_left, rolled(edge_in[n, 1], 32) * has_right)
        carry = lax.fori_loop(0, 6, body, carry)
        edge_copy(n, 2).wait_recv()
        edge_copy(n, 3).wait_recv()
        for g in range(MASS):
            bins = slice(g * RANGE, (g + 1) * RANGE)
            field[0, bins] = jnp.where(
                block == 0, rolled(edge_in[n, 2], -32 * g), rolled(field[ROWS, bins], 32)
            )
            field[ROWS + 1, bins] = jnp.where(
                block == 3, rolled(edge_in[n, 3], 32 * (3 - g)), rolled(field[1, bins], -32)
            )
        lax.fori_loop(6, 8, body, carry)

    def add_product(ah, value, other):
        summed = jnp.sum((value * other).reshape(-1, 8, LANES), axis=0)
        acc[...] += slopes[pl.ds(ah, 1)] * summed

    def arrived(copy):
        def wait(ah):
            for k in (1, 2, 3):
                copy(k, ah).wait_recv()

        return wait

    acc[...] = jnp.zeros((8, LANES), F32)

    def keep_f2(ah, x, frags):
        f2[ah] = frags

    mix(0, cot, back, BACK, w2, arrived(cot_copy), keep_f2)
    lax.fori_loop(EARLY, ROWS, send_m1, 0)

    for k in (1, 2, 3):
        coef_copy(k).wait_recv()
    for g in range(MASS):
        bins = slice(g * RANGE, (g + 1) * RANGE)
        turns = [rolled(coef_in[bins], 32 * k) for k in range(4)]

        def everywhere(source):
            value = turns[(0 - source) % 4]
            for b in (1, 2, 3):
                value = jnp.where(block == b, turns[(b - source) % 4], value)
            return value

        c_in, c_out, c_spread = everywhere(0), everywhere(1), everywhere(2)
        coef[0, bins] = c_in
        coef[1, bins] = c_out
        coef[2, bins] = c_spread
        coef[3, bins] = 1.0 - c_in - c_out - 2.0 * c_spread

    def keep_a1(ah, bins, value):
        a1[ah, bins] = value

    stencil(0, w2, BACK, keep_a1)

    def keep_f1(ah, x, frags):
        f1[ah] = frags

    mix(1, a1, back, BACK, w1, lambda ah: None, keep_f1)

    def first_product(ah, x, frags):
        add_product(ah, x, f1[ah])

    mix(3, m1, forth, FORTH, st, arrived(m1_copy), first_product)

    def keep_res(ah, bins, value):
        res[ah, bins] = value

    def send_row(ah):
        for k in (1, 2, 3):
            ret_copy(k, ah).start()
        ret[m, ah] = res[ah, own]

    stencil(1, w1, BACK, keep_res, send_row)

    def second_product(ah, bins, value):
        add_product(ah, value, f2[ah, bins])

    stencil(3, st, FORTH, second_product)

    flat_out = out.reshape(RANGE * 32, LANES)

    def unpack(i, carry):
        ah = lax.rem(14 - i, 8)
        arrived(ret_copy)(ah)
        tiles = swap_blocks([ret[k, ah] for k in range(MASS)])
        for al in range(4):
            flat_out[pl.ds(al * 8 + ah, RANGE, stride=32), :] = tiles[al]
        return carry

    total = jnp.sum(acc[...], axis=0, keepdims=True)
    total = total + rolled(total, 32) + rolled(total, 64) + rolled(total, 96)
    total = jnp.broadcast_to(total, (8, LANES))
    total = jnp.where(block8 == m, total, 0.0)
    for n, (place, peer) in enumerate(((low, low_peer), (corner, corner_peer))):
        red[n, place] = total
        copies = []
        for k in range(1, 8):
            copies.append(
                pltpu.make_async_remote_copy(
                    src_ref=red.at[n, place],
                    dst_ref=red.at[n, place],
                    send_sem=red_send.at[n, k - 1],
                    recv_sem=red_recv.at[n, k - 1],
                    device_id=peer(k),
                    device_id_type=MESH,
                )
            )
        for copy in copies:
            copy.start()
        lax.fori_loop(4 * n, 4 * n + 4, unpack, 0)
        for copy in copies:
            copy.wait()
        total = ((red[n, 0] + red[n, 1]) + (red[n, 2] + red[n, 3])) + (
            (red[n, 4] + red[n, 5]) + (red[n, 6] + red[n, 7])
        )
    grad[...] = total[0:1]

    def drain(ah, carry):
        for copy in (cot_copy, m1_copy, ret_copy):
            for k in (1, 2, 3):
                copy(k, ah).wait_send()
        return carry

    lax.fori_loop(0, ROWS, drain, 0)
    for k in (1, 2, 3):
        coef_copy(k).wait_send()
    for n in range(4):
        for i in range(4):
            edge_copy(n, i).wait_send()


def per_device(
    density,
    cotangent,
    drift_in,
    drift_out,
    spread,
    dest_bins,
    bott_split,
    coag_rate,
    frag_pairs,
    frag_gain,
    frag_rate,
    collide_speed,
    frag_speed,
    regime,
):
    keep = lambda v: pltpu.with_memory_space_constraint(v, pltpu.HBM)
    vmem = pl.BlockSpec(memory_space=pltpu.VMEM)
    hbm = pl.BlockSpec(memory_space=pltpu.HBM)
    field = pltpu.VMEM((ROWS, BINS, LANES), F32)
    padded = pltpu.VMEM((ROWS + 2, BINS, LANES), F32)
    packed = pltpu.VMEM((MASS, ROWS, RANGE, LANES), F32)
    raw = pltpu.VMEM(density.shape, F32)
    matrix = pltpu.VMEM((2 * BINS, 3 * BINS), BF16)
    small = pltpu.VMEM((ROWS, LANES), F32)
    edges = pltpu.VMEM((4, 4, RANGE, LANES), F32)
    tile = pltpu.VMEM((RANGE, LANES), F32)
    per_bin = pltpu.VMEM((1, BINS), F32)
    cells = pltpu.VMEM((32, LANES), F32)
    dma = pltpu.SemaphoreType.DMA
    adjoint, gradient = pl.pallas_call(
        kernel,
        out_shape=(
            jax.ShapeDtypeStruct(density.shape, F32),
            jax.ShapeDtypeStruct((1, LANES), F32),
        ),
        in_specs=[hbm] * 14,
        out_specs=(vmem, vmem),
        scratch_shapes=[
            pltpu.SMEM((MASS, MASS), jnp.int32),
            raw,
            raw,
            tile,
            tile,
            pltpu.VMEM((1, RANGE), F32),
            pltpu.VMEM((1, BINS), jnp.int32),
            per_bin,
            per_bin,
            pltpu.VMEM((BINS, BINS), F32),
            per_bin,
            cells,
            pltpu.VMEM((1, LANES), F32),
            pltpu.VMEM((32, LANES), jnp.int32),
            pltpu.VMEM((34, RANGE, LANES), F32),
            pltpu.VMEM((2, RANGE, LANES), F32),
            pltpu.VMEM((32, RANGE, LANES), F32),
            packed,
            packed,
            field,
            field,
            pltpu.VMEM((MASS, RANGE, LANES), F32),
            pltpu.VMEM((BINS, LANES), F32),
            pltpu.VMEM((4, BINS, LANES), F32),
            matrix,
            matrix,
            small,
            small,
            padded,
            field,
            field,
            padded,
            field,
            padded,
            field,
            packed,
            edges,
            edges,
            small,
            pltpu.VMEM((2, 8, ROWS, LANES), F32),
            dma((14,)),
            dma((3, 3, ROWS)),
            dma((3, 3, ROWS)),
            dma((3,)),
            dma((3,)),
            dma((4, 4)),
            dma((4, 4)),
            dma((2, 7)),
            dma((2, 7)),
        ],
        compiler_params=pltpu.CompilerParams(
            collective_id=0, has_side_effects=True, vmem_limit_bytes=48 << 20
        ),
    )(keep(frag_pairs), keep(density), keep(cotangent), keep(drift_in), keep(drift_out), keep(spread[None, :]), keep(dest_bins[None, :]), keep(bott_split[None, :]), keep(coag_rate[None, :]), keep(frag_gain), keep(frag_rate[None, :]), keep(collide_speed), keep(frag_speed[None, :]), keep(regime))
    return adjoint, gradient[0]


def solution(mesh):
    in_specs = (
        P("mass", "phi", "row"),
        P("mass", "phi", "row"),
        P("mass", None),
        P("mass", None),
        P("mass"),
        P(),
        P(),
        P(),
        P(),
        P(),
        P(),
        P("phi", "row"),
        P("row"),
        P("phi", "row"),
    )
    out_specs = (P("mass", "phi", "row"), P("row"))
    return jax.shard_map(
        per_device, mesh=mesh, in_specs=in_specs, out_specs=out_specs, check_vma=False
    )
```

```python
import functools

import jax
import jax.numpy as jnp
from jax import lax
from jax.experimental import pallas as pl
from jax.experimental.pallas import tpu as pltpu
from jax.sharding import PartitionSpec as P


MESH = pl.DeviceIdType.MESH
F32 = jnp.float32
BF16 = jnp.bfloat16
RANGE = 64
MASS = 4
ROWS = 8
BINS = 256
LANES = 128
GATE_WIDTH = 0.5
BACK, FORTH = 0, 1
EARLY = 2


def lanes_of(shape):
    return lax.broadcasted_iota(jnp.int32, shape, len(shape) - 1)


def rolled(value, shift):
    shift = shift % LANES
    return value if shift == 0 else pltpu.roll(value, shift, value.ndim - 1)


def swap_blocks(tiles):
    block = lanes_of(tiles[0].shape) // 32
    low = block < 2
    even = block % 2 == 0
    s0, s1, s2, s3 = tiles
    a0 = jnp.where(low, s0, rolled(s2, 64))
    a2 = jnp.where(low, rolled(s0, 64), s2)
    a1 = jnp.where(low, s1, rolled(s3, 64))
    a3 = jnp.where(low, rolled(s1, 64), s3)
    return (
        jnp.where(even, a0, rolled(a1, 32)),
        jnp.where(even, rolled(a0, 96), a1),
        jnp.where(even, a2, rolled(a3, 32)),
        jnp.where(even, rolled(a2, 96), a3),
    )


def high_low(value):
    high = value.astype(BF16)
    return high, (value - high.astype(F32)).astype(BF16)


def kernel(
    pairs_hbm,
    density,
    cotangent,
    drift_in,
    drift_out,
    spread_hbm,
    dest_hbm,
    split_hbm,
    rate_hbm,
    gain_hbm,
    frag_rate_hbm,
    speed_hbm,
    frag_speed_hbm,
    regime_hbm,
    out,
    grad,
    pairs,
    raw_c,
    raw_d,
    in_q,
    out_q,
    spread,
    dest,
    split,
    rate,
    gain,
    frag_rate,
    speed,
    frag_speed,
    regime,
    here,
    own_coef,
    there,
    pack_c,
    pack_d,
    cot,
    m1,
    coef_out,
    coef_part,
    coef_all,
    coef,
    back,
    forth,
    gates,
    slopes,
    w2,
    f2,
    a1,
    w1,
    f1,
    st,
    res,
    ret,
    edge_out,
    edge_in,
    acc,
    red,
    load_sem,
    field_send,
    field_recv,
    coef_send,
    coef_recv,
    share_send,
    share_recv,
    edge_send,
    edge_recv,
    red_send,
    red_recv,
):
    phi = lax.axis_index("phi")
    row = lax.axis_index("row")
    m = lax.axis_index("mass")
    phis = lax.axis_size("phi")
    rows = lax.axis_size("row")
    low = lax.rem(phi, 8)
    high = phi // 8
    corner = high * MASS + m

    at = pl.multiple_of(row * LANES, LANES)
    sources = (
        (cotangent, raw_c),
        (spread_hbm, spread),
        (drift_in.at[:, pl.ds(at, LANES)], in_q),
        (drift_out.at[:, pl.ds(at, LANES)], out_q),
        (density, raw_d),
        (dest_hbm, dest),
        (split_hbm, split),
        (rate_hbm, rate),
        (gain_hbm, gain),
        (frag_rate_hbm, frag_rate),
        (pairs_hbm, pairs),
        (speed_hbm, speed),
        (frag_speed_hbm, frag_speed),
        (regime_hbm, regime),
    )
    loads = [pltpu.make_async_copy(x, y, load_sem.at[i]) for i, (x, y) in enumerate(sources)]
    for load in loads[:4]:
        load.start()

    def mass_peer(k):
        return {"mass": lax.rem(m + k, MASS)}

    def low_peer(k):
        return {"phi": high * 8 + lax.rem(low + k, 8)}

    def corner_peer(k):
        other = lax.rem(corner + k, 8)
        return {"phi": (other // MASS) * 8 + low, "mass": lax.rem(other, MASS)}

    radial = row * MASS + m
    radials = rows * MASS
    right_at = lax.rem(radial + 1, radials)
    left_at = lax.rem(radial + radials - 1, radials)
    right = {"row": right_at // MASS, "mass": lax.rem(right_at, MASS)}
    left = {"row": left_at // MASS, "mass": lax.rem(left_at, MASS)}
    row_right = {"row": lax.rem(row + 1, rows)}
    row_left = {"row": lax.rem(row + rows - 1, rows)}
    after = {"phi": lax.rem(phi + 1, phis)}
    before = {"phi": lax.rem(phi + phis - 1, phis)}

    barrier = pltpu.get_barrier_semaphore()
    greeted = [mass_peer(k) for k in (1, 2, 3)]
    greeted += [right, left, row_right, row_left, after, before]
    greeted += [low_peer(k) for k in range(1, 8)] + [corner_peer(k) for k in range(1, 8)]
    for device in greeted:
        pl.semaphore_signal(barrier, inc=1, device_id=device, device_id_type=MESH)

    tile = (RANGE, LANES)
    lane = lanes_of(tile)
    block = lane // 32
    within = lax.rem(lane, 32)
    first = within == 0
    final = within == 31
    zero = jnp.zeros(tile, F32)

    def field_copy(kind, k, ah, source, target):
        return pltpu.make_async_remote_copy(
            src_ref=source,
            dst_ref=target,
            send_sem=field_send.at[kind, k - 1, ah],
            recv_sem=field_recv.at[kind, k - 1, ah],
            device_id=mass_peer(k),
            device_id_type=MESH,
        )

    own = pl.ds(pl.multiple_of(m * RANGE, RANGE), RANGE)

    def cot_copy(k, ah):
        return field_copy(0, k, ah, pack_c.at[lax.rem(m + k, MASS), ah], cot.at[ah, own])

    def m1_copy(k, ah):
        return field_copy(1, k, ah, pack_d.at[lax.rem(m + k, MASS), ah], m1.at[ah, own])

    def ret_copy(k, ah):
        theirs = pl.ds(pl.multiple_of(lax.rem(m + k, MASS) * RANGE, RANGE), RANGE)
        return field_copy(2, k, ah, res.at[ah, theirs], ret.at[m, ah])

    eighth = pl.ds(pl.multiple_of(low * 8, 8), 8)

    def coef_copy(k):
        return pltpu.make_async_remote_copy(
            src_ref=coef_out.at[lax.rem(m + k, MASS), eighth],
            dst_ref=coef_part.at[m],
            send_sem=coef_send.at[k - 1],
            recv_sem=coef_recv.at[k - 1],
            device_id=mass_peer(k),
            device_id_type=MESH,
        )

    def share_copy(k):
        return pltpu.make_async_remote_copy(
            src_ref=coef_part,
            dst_ref=coef_all.at[low],
            send_sem=share_send.at[k - 1],
            recv_sem=share_recv.at[k - 1],
            device_id=low_peer(k),
            device_id_type=MESH,
        )

    def edge_copy(n, i):
        device = ((row_right, row_left) if n == 2 else (right, left)) + (after, before)
        return pltpu.make_async_remote_copy(
            src_ref=edge_out.at[n, i],
            dst_ref=edge_in.at[n, i],
            send_sem=edge_send.at[n, i],
            recv_sem=edge_recv.at[n, i],
            device_id=device[i],
            device_id_type=MESH,
        )

    for i in (1, 2, 3):
        loads[i].wait()
    square = (RANGE, RANGE)
    on_diag = lax.broadcasted_iota(jnp.int32, square, 0) == lanes_of(square)
    spread_col = jnp.sum(jnp.where(on_diag, jnp.broadcast_to(spread[...], square), 0.0), axis=1, keepdims=True)
    spread_tile = jnp.broadcast_to(spread_col, tile)
    for k in range(MASS):
        coef_out[k] = jnp.where(
            block == 0,
            rolled(in_q[...], -32 * k),
            jnp.where(block == 1, rolled(out_q[...], 32 - 32 * k), spread_tile),
        )
    coef_part[m] = coef_out[m, eighth]
    own_coef[0] = 1.0 - in_q[...] - out_q[...] - 2.0 * spread_tile
    own_coef[1] = spread_tile

    flat_c = raw_c.reshape(RANGE * 32, LANES)

    def send_cot(i, carry):
        ah = lax.rem(i + 7, 8)
        tiles = swap_blocks([flat_c[pl.ds(al * 8 + ah, RANGE, stride=32), :] for al in range(4)])
        for k in range(MASS):
            pack_c[k, ah] = tiles[k]
        for k in (1, 2, 3):
            cot_copy(k, ah).start()
        cot[ah, own] = pack_c[m, ah]
        return carry

    loads[0].wait()
    for load in loads[4:]:
        load.start()
    pl.semaphore_wait(barrier, len(greeted))
    for k in (1, 2, 3):
        coef_copy(k).start()
    lax.fori_loop(0, ROWS, send_cot, 0)

    loads[4].wait()
    flat_d = raw_d.reshape(RANGE * 32, LANES)
    edge_out[2, 2] = flat_d[pl.ds(31, RANGE, stride=32), :]
    edge_out[2, 3] = flat_d[pl.ds(0, RANGE, stride=32), :]
    edge_copy(2, 2).start()
    edge_copy(2, 3).start()
    lowest = lane == 0
    topmost = lane == LANES - 1

    def own_edges(i, carry):
        last_col, first_col = rolled(carry[0], -4), rolled(carry[1], 4)
        for k in range(4):
            a = i * 4 + k
            value = flat_d[pl.ds(a, RANGE, stride=32), :]
            here[a + 1] = value
            last_col = jnp.where(lane == LANES - 4 + k, rolled(out_q[...] * value, k - 3), last_col)
            first_col = jnp.where(lane == 3 - k, rolled(in_q[...] * value, 3 - k), first_col)
        return last_col, first_col

    last_col, first_col = lax.fori_loop(0, 8, own_edges, (zero, zero))
    edge_out[2, 0] = last_col
    edge_out[2, 1] = first_col
    edge_copy(2, 0).start()
    edge_copy(2, 1).start()
    for k in (1, 2, 3):
        coef_copy(k).wait_recv()
    for k in range(1, 8):
        share_copy(k).start()
    coef_all[low] = coef_part[...]

    for load in loads[5:]:
        load.wait()
    whole = (BINS, BINS)
    row_ids = lax.broadcasted_iota(jnp.int32, whole, 0)
    col_ids = lanes_of(whole)
    target = jnp.broadcast_to(dest[...], whole)
    upper = jnp.broadcast_to(split[...], whole)
    diag = jnp.where(row_ids == col_ids, 1.0, 0.0)
    coag_full = (
        jnp.where(row_ids == target, 1.0 - upper, 0.0) + jnp.where(row_ids == target + 1, upper, 0.0) - diag
    ) * rate[...]
    strip = (RANGE, BINS)
    strip_block = lanes_of(strip) // RANGE
    chosen = []
    for i in range(MASS):
        line = jnp.zeros(strip, F32)
        for j in range(MASS):
            line = jnp.where(strip_block == j, pairs[i, j].astype(F32), line)
        chosen.append(line)
    chosen = jnp.concatenate(chosen, axis=0)
    frag_full = gain[...] * chosen * jnp.where(row_ids <= col_ids, 1.0, 0.0) - diag * frag_rate[...]
    for at_row, matrix in ((0, coag_full), (BINS, frag_full)):
        for kept, value in ((forth, matrix), (back, matrix.T)):
            hi, lo = high_low(value)
            kept[at_row : at_row + BINS, 0:BINS] = hi
            kept[at_row : at_row + BINS, BINS : 2 * BINS] = hi
            kept[at_row : at_row + BINS, 2 * BINS : 3 * BINS] = lo

    sigma = 1.0 / (1.0 + jnp.exp(-((speed[...] - frag_speed[...]) / GATE_WIDTH)))
    flagged = regime[...].astype(F32)
    gate_all = flagged * sigma
    slope_all = -flagged * sigma * (1.0 - sigma) / GATE_WIDTH
    block8 = lanes_of((ROWS, LANES)) // 32
    for source, kept in ((gate_all, gates), (slope_all, slopes)):
        value = jnp.zeros((ROWS, LANES), F32)
        for al in range(4):
            part = pltpu.roll(source[al * 8 : al * 8 + 8], lax.rem(32 * (al + MASS - m), LANES), 1)
            value = jnp.where(block8 == al, part, value)
        kept[...] = value

    for i in range(4):
        edge_copy(2, i).wait_recv()
    here[0] = edge_in[2, 2]
    here[33] = edge_in[2, 3]
    row_has_left = jnp.where(row > 0, 1.0, 0.0)
    row_has_right = jnp.where(row < rows - 1, 1.0, 0.0)

    def own_forward(i, carry):
        last_col, first_col = carry
        for k in range(4):
            a = i * 4 + k
            value = here[a + 1]
            beside = here[a] + here[a + 2]
            outer = jnp.where(topmost, rolled(first_col, k), rolled(in_q[...] * value, -1))
            inner = jnp.where(lowest, rolled(last_col, -k), rolled(out_q[...] * value, 1))
            there[a] = own_coef[0] * value + outer + inner + own_coef[1] * beside
        return rolled(last_col, -4), rolled(first_col, 4)

    lax.fori_loop(
        0,
        8,
        own_forward,
        (rolled(edge_in[2, 0], 32) * row_has_left, rolled(edge_in[2, 1], 96) * row_has_right),
    )

    def pack_m1(ah, carry):
        tiles = swap_blocks([there[al * 8 + ah] for al in range(4)])
        for k in range(MASS):
            pack_d[k, ah] = tiles[k]
        m1[ah, own] = pack_d[m, ah]
        return carry

    lax.fori_loop(0, ROWS, pack_m1, 0)

    def send_m1(i, carry):
        for k in (1, 2, 3):
            m1_copy(k, lax.rem(i + 7, 8)).start()
        return carry

    lax.fori_loop(0, EARLY, send_m1, 0)

    has_left = jnp.where(radial > 0, 1.0, 0.0)
    has_right = jnp.where(radial < radials - 1, 1.0, 0.0)

    def mix(n, source, matrix, way, state, arrive, seen):
        edge_out[n, 0] = zero
        edge_out[n, 1] = zero

        def body(j, carry):
            pair = (lax.rem(2 * j + 7, 8), 2 * j)
            for ah in pair:
                arrive(ah)
            x = jnp.concatenate([source[ah] for ah in pair], axis=1)
            x_hi, x_lo = high_low(x)
            xc = jnp.concatenate([x_hi, x_lo, x_hi], axis=0)
            gate = jnp.concatenate([gates[pl.ds(ah, 1)] for ah in pair], axis=1)
            news = []
            yfs = []
            for c in range(2):
                part = slice(c * 128, c * 128 + 128)
                yf = jnp.dot(matrix[BINS + c * 128 : BINS + c * 128 + 128], xc, preferred_element_type=F32)
                news.append(x[part] + jnp.dot(matrix[part], xc, preferred_element_type=F32) + gate * yf)
                yfs.append(yf)
            new = jnp.concatenate(news, axis=0)
            frags = jnp.concatenate(yfs, axis=0)
            last_col = rolled(edge_out[n, 0], -8)
            first_col = rolled(edge_out[n, 1], 8)
            for half, ah in enumerate(pair):
                lanes = slice(half * LANES, (half + 1) * LANES)
                state[ah + 1] = new[:, lanes]
                seen(ah, x[:, lanes], frags[:, lanes])
                for g in range(MASS):
                    bins = slice(g * RANGE, (g + 1) * RANGE)
                    value = new[bins, lanes]
                    to_left = value * coef[0, bins] if way == FORTH else value
                    to_right = value * coef[1, bins] if way == FORTH else value
                    u = half * MASS + g
                    last_col = jnp.where(within == 24 + u, rolled(to_right, u - 7), last_col)
                    first_col = jnp.where(within == 7 - u, rolled(to_left, 7 - u), first_col)
            edge_out[n, 0] = last_col
            edge_out[n, 1] = first_col

            @pl.when(j == 0)
            def _():
                for i, ah in ((2, ROWS), (3, 1)):
                    value = zero
                    for g in range(MASS):
                        bins = slice(g * RANGE, (g + 1) * RANGE)
                        part = rolled(state[ah, bins], 32 * (g - 3) if i == 2 else 32 * g)
                        value = jnp.where(block == g, part, value)
                    edge_out[n, i] = value
                    edge_copy(n, i).start()

            return carry

        lax.fori_loop(0, ROWS // 2, body, 0)
        edge_copy(n, 0).start()
        edge_copy(n, 1).start()

    def stencil(n, field, way, emit, after_row=None):
        edge_copy(n, 0).wait_recv()
        edge_copy(n, 1).wait_recv()

        def body(i, carry):
            last_col, first_col = carry
            ah = lax.rem(14 - i, 8)
            for t in range(MASS):
                g = MASS - 1 - t
                bins = slice(g * RANGE, (g + 1) * RANGE)
                value = field[ah + 1, bins]
                beside = field[ah, bins] + field[ah + 2, bins]
                c_in, c_out = coef[0, bins], coef[1, bins]
                to_left = c_in * value if way == FORTH else value
                to_right = c_out * value if way == FORTH else value
                outer = rolled(jnp.where(first, rolled(first_col, -t), to_left), -1)
                inner = rolled(jnp.where(final, rolled(last_col, t), to_right), 1)
                both = outer + inner if way == FORTH else c_in * inner + c_out * outer
                emit(ah, bins, coef[3, bins] * value + both + coef[2, bins] * beside)
            last_col = rolled(last_col, MASS)
            first_col = rolled(first_col, -MASS)
            if after_row is not None:
                after_row(ah)
            return last_col, first_col

        carry = (rolled(edge_in[n, 0], -32) * has_left, rolled(edge_in[n, 1], 32) * has_right)
        carry = lax.fori_loop(0, 6, body, carry, unroll=2)
        edge_copy(n, 2).wait_recv()
        edge_copy(n, 3).wait_recv()
        for g in range(MASS):
            bins = slice(g * RANGE, (g + 1) * RANGE)
            field[0, bins] = jnp.where(
                block == 0, rolled(edge_in[n, 2], -32 * g), rolled(field[ROWS, bins], 32)
            )
            field[ROWS + 1, bins] = jnp.where(
                block == 3, rolled(edge_in[n, 3], 32 * (3 - g)), rolled(field[1, bins], -32)
            )
        lax.fori_loop(6, 8, body, carry, unroll=True)

    def add_product(ah, value, other):
        summed = jnp.sum((value * other).reshape(-1, 8, LANES), axis=0)
        acc[...] += slopes[pl.ds(ah, 1)] * summed

    def arrived(copy):
        def wait(ah):
            for k in (1, 2, 3):
                copy(k, ah).wait_recv()

        return wait

    acc[...] = jnp.zeros((8, LANES), F32)

    def keep_f2(ah, x, frags):
        f2[ah] = frags

    mix(0, cot, back, BACK, w2, arrived(cot_copy), keep_f2)
    lax.fori_loop(EARLY, ROWS, send_m1, 0)

    for k in range(1, 8):
        share_copy(k).wait_recv()
    for g in range(MASS):
        bins = slice(g * RANGE, (g + 1) * RANGE)
        sent = jnp.concatenate([coef_all[i, g] for i in range(8)], axis=0)
        turns = [rolled(sent, 32 * k) for k in range(4)]

        def everywhere(source):
            value = turns[(0 - source) % 4]
            for b in (1, 2, 3):
                value = jnp.where(block == b, turns[(b - source) % 4], value)
            return value

        c_in, c_out, c_spread = everywhere(0), everywhere(1), everywhere(2)
        coef[0, bins] = c_in
        coef[1, bins] = c_out
        coef[2, bins] = c_spread
        coef[3, bins] = 1.0 - c_in - c_out - 2.0 * c_spread

    def keep_a1(ah, bins, value):
        a1[ah, bins] = value

    stencil(0, w2, BACK, keep_a1)

    def keep_f1(ah, x, frags):
        f1[ah] = frags

    mix(1, a1, back, BACK, w1, lambda ah: None, keep_f1)

    def first_product(ah, x, frags):
        add_product(ah, x, f1[ah])

    mix(3, m1, forth, FORTH, st, arrived(m1_copy), first_product)

    def keep_res(ah, bins, value):
        res[ah, bins] = value

    def send_row(ah):
        for k in (1, 2, 3):
            ret_copy(k, ah).start()
        ret[m, ah] = res[ah, own]

    stencil(1, w1, BACK, keep_res, send_row)

    def second_product(ah, bins, value):
        add_product(ah, value, f2[ah, bins])

    stencil(3, st, FORTH, second_product)

    flat_out = out.reshape(RANGE * 32, LANES)

    def unpack(i, carry):
        ah = lax.rem(14 - i, 8)
        arrived(ret_copy)(ah)
        tiles = swap_blocks([ret[k, ah] for k in range(MASS)])
        for al in range(4):
            flat_out[pl.ds(al * 8 + ah, RANGE, stride=32), :] = tiles[al]
        return carry

    total = jnp.sum(acc[...], axis=0, keepdims=True)
    total = total + rolled(total, 32) + rolled(total, 64) + rolled(total, 96)
    total = jnp.broadcast_to(total, (8, LANES))
    total = jnp.where(block8 == m, total, 0.0)
    for n, (place, peer) in enumerate(((low, low_peer), (corner, corner_peer))):
        red[n, place] = total
        copies = []
        for k in range(1, 8):
            copies.append(
                pltpu.make_async_remote_copy(
                    src_ref=red.at[n, place],
                    dst_ref=red.at[n, place],
                    send_sem=red_send.at[n, k - 1],
                    recv_sem=red_recv.at[n, k - 1],
                    device_id=peer(k),
                    device_id_type=MESH,
                )
            )
        for copy in copies:
            copy.start()
        lax.fori_loop(4 * n, 4 * n + 4, unpack, 0)
        for copy in copies:
            copy.wait()
        total = ((red[n, 0] + red[n, 1]) + (red[n, 2] + red[n, 3])) + (
            (red[n, 4] + red[n, 5]) + (red[n, 6] + red[n, 7])
        )
    grad[...] = total[0:1]

    def drain(ah, carry):
        for copy in (cot_copy, m1_copy, ret_copy):
            for k in (1, 2, 3):
                copy(k, ah).wait_send()
        return carry

    lax.fori_loop(0, ROWS, drain, 0)
    for k in (1, 2, 3):
        coef_copy(k).wait_send()
    for k in range(1, 8):
        share_copy(k).wait_send()
    for n in range(4):
        for i in range(4):
            edge_copy(n, i).wait_send()


def per_device(
    density,
    cotangent,
    drift_in,
    drift_out,
    spread,
    dest_bins,
    bott_split,
    coag_rate,
    frag_pairs,
    frag_gain,
    frag_rate,
    collide_speed,
    frag_speed,
    regime,
):
    keep = lambda v: pltpu.with_memory_space_constraint(v, pltpu.HBM)
    vmem = pl.BlockSpec(memory_space=pltpu.VMEM)
    hbm = pl.BlockSpec(memory_space=pltpu.HBM)
    field = pltpu.VMEM((ROWS, BINS, LANES), F32)
    padded = pltpu.VMEM((ROWS + 2, BINS, LANES), F32)
    packed = pltpu.VMEM((MASS, ROWS, RANGE, LANES), F32)
    raw = pltpu.VMEM(density.shape, F32)
    matrix = pltpu.VMEM((2 * BINS, 3 * BINS), BF16)
    small = pltpu.VMEM((ROWS, LANES), F32)
    edges = pltpu.VMEM((4, 4, RANGE, LANES), F32)
    tile = pltpu.VMEM((RANGE, LANES), F32)
    per_bin = pltpu.VMEM((1, BINS), F32)
    cells = pltpu.VMEM((32, LANES), F32)
    dma = pltpu.SemaphoreType.DMA
    adjoint, gradient = pl.pallas_call(
        kernel,
        out_shape=(
            jax.ShapeDtypeStruct(density.shape, F32),
            jax.ShapeDtypeStruct((1, LANES), F32),
        ),
        in_specs=[hbm] * 14,
        out_specs=(vmem, vmem),
        scratch_shapes=[
            pltpu.SMEM((MASS, MASS), jnp.int32),
            raw,
            raw,
            tile,
            tile,
            pltpu.VMEM((1, RANGE), F32),
            pltpu.VMEM((1, BINS), jnp.int32),
            per_bin,
            per_bin,
            pltpu.VMEM((BINS, BINS), F32),
            per_bin,
            cells,
            pltpu.VMEM((1, LANES), F32),
            pltpu.VMEM((32, LANES), jnp.int32),
            pltpu.VMEM((34, RANGE, LANES), F32),
            pltpu.VMEM((2, RANGE, LANES), F32),
            pltpu.VMEM((32, RANGE, LANES), F32),
            packed,
            packed,
            field,
            field,
            pltpu.VMEM((MASS, RANGE, LANES), F32),
            pltpu.VMEM((MASS, 8, LANES), F32),
            pltpu.VMEM((8, MASS, 8, LANES), F32),
            pltpu.VMEM((4, BINS, LANES), F32),
            matrix,
            matrix,
            small,
            small,
            padded,
            field,
            field,
            padded,
            field,
            padded,
            field,
            packed,
            edges,
            edges,
            small,
            pltpu.VMEM((2, 8, ROWS, LANES), F32),
            dma((14,)),
            dma((3, 3, ROWS)),
            dma((3, 3, ROWS)),
            dma((3,)),
            dma((3,)),
            dma((7,)),
            dma((7,)),
            dma((4, 4)),
            dma((4, 4)),
            dma((2, 7)),
            dma((2, 7)),
        ],
        compiler_params=pltpu.CompilerParams(
            collective_id=0, has_side_effects=True, vmem_limit_bytes=48 << 20
        ),
    )(keep(frag_pairs), keep(density), keep(cotangent), keep(drift_in), keep(drift_out), keep(spread[None, :]), keep(dest_bins[None, :]), keep(bott_split[None, :]), keep(coag_rate[None, :]), keep(frag_gain), keep(frag_rate[None, :]), keep(collide_speed), keep(frag_speed[None, :]), keep(regime))
    return adjoint, gradient[0]


def solution(mesh):
    in_specs = (
        P("mass", "phi", "row"),
        P("mass", "phi", "row"),
        P("mass", None),
        P("mass", None),
        P("mass"),
        P(),
        P(),
        P(),
        P(),
        P(),
        P(),
        P("phi", "row"),
        P("row"),
        P("phi", "row"),
    )
    out_specs = (P("mass", "phi", "row"), P("row"))
    return jax.shard_map(
        per_device, mesh=mesh, in_specs=in_specs, out_specs=out_specs, check_vma=False
    )
```

```python
import functools

import jax
import jax.numpy as jnp
from jax import lax
from jax.experimental import pallas as pl
from jax.experimental.pallas import tpu as pltpu
from jax.sharding import PartitionSpec as P


MESH = pl.DeviceIdType.MESH
F32 = jnp.float32
BF16 = jnp.bfloat16
RANGE = 64
MASS = 4
ROWS = 8
BINS = 256
LANES = 128
GATE_WIDTH = 0.5
BACK, FORTH = 0, 1
EARLY = 2


def lanes_of(shape):
    return lax.broadcasted_iota(jnp.int32, shape, len(shape) - 1)


def rolled(value, shift):
    shift = shift % LANES
    return value if shift == 0 else pltpu.roll(value, shift, value.ndim - 1)


def swap_blocks(tiles):
    block = lanes_of(tiles[0].shape) // 32
    low = block < 2
    even = block % 2 == 0
    s0, s1, s2, s3 = tiles
    a0 = jnp.where(low, s0, rolled(s2, 64))
    a2 = jnp.where(low, rolled(s0, 64), s2)
    a1 = jnp.where(low, s1, rolled(s3, 64))
    a3 = jnp.where(low, rolled(s1, 64), s3)
    return (
        jnp.where(even, a0, rolled(a1, 32)),
        jnp.where(even, rolled(a0, 96), a1),
        jnp.where(even, a2, rolled(a3, 32)),
        jnp.where(even, rolled(a2, 96), a3),
    )


def high_low(value):
    high = value.astype(BF16)
    return high, (value - high.astype(F32)).astype(BF16)


def kernel(
    pairs_hbm,
    density,
    cotangent,
    drift_in,
    drift_out,
    spread_hbm,
    dest_hbm,
    split_hbm,
    rate_hbm,
    gain_hbm,
    frag_rate_hbm,
    speed_hbm,
    frag_speed_hbm,
    regime_hbm,
    out,
    grad,
    pairs,
    raw_c,
    raw_d,
    in_q,
    out_q,
    spread,
    dest,
    split,
    rate,
    gain,
    frag_rate,
    speed,
    frag_speed,
    regime,
    here,
    own_coef,
    there,
    pack_c,
    pack_d,
    cot,
    m1,
    coef_out,
    coef_part,
    coef_all,
    coef,
    back,
    forth,
    gates,
    slopes,
    w2,
    f2,
    a1,
    w1,
    f1,
    st,
    res,
    ret,
    edge_out,
    edge_in,
    acc,
    red,
    load_sem,
    field_send,
    field_recv,
    coef_send,
    coef_recv,
    share_send,
    share_recv,
    edge_send,
    edge_recv,
    red_send,
    red_recv,
):
    phi = lax.axis_index("phi")
    row = lax.axis_index("row")
    m = lax.axis_index("mass")
    phis = lax.axis_size("phi")
    rows = lax.axis_size("row")
    low = lax.rem(phi, 8)
    high = phi // 8
    corner = high * MASS + m

    at = pl.multiple_of(row * LANES, LANES)
    sources = (
        (cotangent, raw_c),
        (spread_hbm, spread),
        (drift_in.at[:, pl.ds(at, LANES)], in_q),
        (drift_out.at[:, pl.ds(at, LANES)], out_q),
        (density, raw_d),
        (dest_hbm, dest),
        (split_hbm, split),
        (rate_hbm, rate),
        (gain_hbm, gain),
        (frag_rate_hbm, frag_rate),
        (pairs_hbm, pairs),
        (speed_hbm, speed),
        (frag_speed_hbm, frag_speed),
        (regime_hbm, regime),
    )
    loads = [pltpu.make_async_copy(x, y, load_sem.at[i]) for i, (x, y) in enumerate(sources)]
    for load in loads[:4]:
        load.start()

    def mass_peer(k):
        return {"mass": lax.rem(m + k, MASS)}

    def low_peer(k):
        return {"phi": high * 8 + lax.rem(low + k, 8)}

    def corner_peer(k):
        other = lax.rem(corner + k, 8)
        return {"phi": (other // MASS) * 8 + low, "mass": lax.rem(other, MASS)}

    radial = row * MASS + m
    radials = rows * MASS
    right_at = lax.rem(radial + 1, radials)
    left_at = lax.rem(radial + radials - 1, radials)
    right = {"row": right_at // MASS, "mass": lax.rem(right_at, MASS)}
    left = {"row": left_at // MASS, "mass": lax.rem(left_at, MASS)}
    row_right = {"row": lax.rem(row + 1, rows)}
    row_left = {"row": lax.rem(row + rows - 1, rows)}
    after = {"phi": lax.rem(phi + 1, phis)}
    before = {"phi": lax.rem(phi + phis - 1, phis)}

    barrier = pltpu.get_barrier_semaphore()
    greeted = [mass_peer(k) for k in (1, 2, 3)]
    greeted += [right, left, row_right, row_left, after, before]
    greeted += [low_peer(k) for k in range(1, 8)] + [corner_peer(k) for k in range(1, 8)]
    for device in greeted:
        pl.semaphore_signal(barrier, inc=1, device_id=device, device_id_type=MESH)

    tile = (RANGE, LANES)
    lane = lanes_of(tile)
    block = lane // 32
    within = lax.rem(lane, 32)
    first = within == 0
    final = within == 31
    zero = jnp.zeros(tile, F32)

    def field_copy(kind, k, ah, source, target):
        return pltpu.make_async_remote_copy(
            src_ref=source,
            dst_ref=target,
            send_sem=field_send.at[kind, k - 1, ah],
            recv_sem=field_recv.at[kind, k - 1, ah],
            device_id=mass_peer(k),
            device_id_type=MESH,
        )

    own = pl.ds(pl.multiple_of(m * RANGE, RANGE), RANGE)

    def cot_copy(k, ah):
        return field_copy(0, k, ah, pack_c.at[lax.rem(m + k, MASS), ah], cot.at[ah, own])

    def m1_copy(k, ah):
        return field_copy(1, k, ah, pack_d.at[lax.rem(m + k, MASS), ah], m1.at[ah, own])

    def ret_copy(k, ah):
        theirs = pl.ds(pl.multiple_of(lax.rem(m + k, MASS) * RANGE, RANGE), RANGE)
        return field_copy(2, k, ah, res.at[ah, theirs], ret.at[m, ah])

    eighth = pl.ds(pl.multiple_of(low * 8, 8), 8)

    def coef_copy(k):
        return pltpu.make_async_remote_copy(
            src_ref=coef_out.at[lax.rem(m + k, MASS), eighth],
            dst_ref=coef_part.at[m],
            send_sem=coef_send.at[k - 1],
            recv_sem=coef_recv.at[k - 1],
            device_id=mass_peer(k),
            device_id_type=MESH,
        )

    def share_copy(k):
        return pltpu.make_async_remote_copy(
            src_ref=coef_part,
            dst_ref=coef_all.at[low],
            send_sem=share_send.at[k - 1],
            recv_sem=share_recv.at[k - 1],
            device_id=low_peer(k),
            device_id_type=MESH,
        )

    def edge_copy(n, i):
        device = ((row_right, row_left) if n == 2 else (right, left)) + (after, before)
        return pltpu.make_async_remote_copy(
            src_ref=edge_out.at[n, i],
            dst_ref=edge_in.at[n, i],
            send_sem=edge_send.at[n, i],
            recv_sem=edge_recv.at[n, i],
            device_id=device[i],
            device_id_type=MESH,
        )

    for i in (1, 2, 3):
        loads[i].wait()
    square = (RANGE, RANGE)
    on_diag = lax.broadcasted_iota(jnp.int32, square, 0) == lanes_of(square)
    spread_col = jnp.sum(jnp.where(on_diag, jnp.broadcast_to(spread[...], square), 0.0), axis=1, keepdims=True)
    spread_tile = jnp.broadcast_to(spread_col, tile)
    for k in range(MASS):
        coef_out[k] = jnp.where(
            block == 0,
            rolled(in_q[...], -32 * k),
            jnp.where(block == 1, rolled(out_q[...], 32 - 32 * k), spread_tile),
        )
    coef_part[m] = coef_out[m, eighth]
    own_coef[0] = 1.0 - in_q[...] - out_q[...] - 2.0 * spread_tile
    own_coef[1] = spread_tile

    flat_c = raw_c.reshape(RANGE * 32, LANES)

    def send_cot(i, carry):
        ah = lax.rem(i + 7, 8)
        tiles = swap_blocks([flat_c[pl.ds(al * 8 + ah, RANGE, stride=32), :] for al in range(4)])
        for k in range(MASS):
            pack_c[k, ah] = tiles[k]
        for k in (1, 2, 3):
            cot_copy(k, ah).start()
        cot[ah, own] = pack_c[m, ah]
        return carry

    loads[0].wait()
    for load in loads[4:]:
        load.start()
    pl.semaphore_wait(barrier, len(greeted))
    for k in (1, 2, 3):
        coef_copy(k).start()
    lax.fori_loop(0, ROWS, send_cot, 0)

    loads[4].wait()
    flat_d = raw_d.reshape(RANGE * 32, LANES)
    edge_out[2, 2] = flat_d[pl.ds(31, RANGE, stride=32), :]
    edge_out[2, 3] = flat_d[pl.ds(0, RANGE, stride=32), :]
    edge_copy(2, 2).start()
    edge_copy(2, 3).start()
    lowest = lane == 0
    topmost = lane == LANES - 1

    def own_edges(i, carry):
        last_col, first_col = rolled(carry[0], -4), rolled(carry[1], 4)
        for k in range(4):
            a = i * 4 + k
            value = flat_d[pl.ds(a, RANGE, stride=32), :]
            here[a + 1] = value
            last_col = jnp.where(lane == LANES - 4 + k, rolled(out_q[...] * value, k - 3), last_col)
            first_col = jnp.where(lane == 3 - k, rolled(in_q[...] * value, 3 - k), first_col)
        return last_col, first_col

    last_col, first_col = lax.fori_loop(0, 8, own_edges, (zero, zero))
    edge_out[2, 0] = last_col
    edge_out[2, 1] = first_col
    edge_copy(2, 0).start()
    edge_copy(2, 1).start()
    for k in (1, 2, 3):
        coef_copy(k).wait_recv()
    for k in range(1, 8):
        share_copy(k).start()
    coef_all[low] = coef_part[...]

    for load in loads[5:]:
        load.wait()
    whole = (BINS, BINS)
    row_ids = lax.broadcasted_iota(jnp.int32, whole, 0)
    col_ids = lanes_of(whole)
    target = jnp.broadcast_to(dest[...], whole)
    upper = jnp.broadcast_to(split[...], whole)
    diag = jnp.where(row_ids == col_ids, 1.0, 0.0)
    coag_full = (
        jnp.where(row_ids == target, 1.0 - upper, 0.0) + jnp.where(row_ids == target + 1, upper, 0.0) - diag
    ) * rate[...]
    strip = (RANGE, BINS)
    strip_block = lanes_of(strip) // RANGE
    chosen = []
    for i in range(MASS):
        line = jnp.zeros(strip, F32)
        for j in range(MASS):
            line = jnp.where(strip_block == j, pairs[i, j].astype(F32), line)
        chosen.append(line)
    chosen = jnp.concatenate(chosen, axis=0)
    frag_full = gain[...] * chosen * jnp.where(row_ids <= col_ids, 1.0, 0.0) - diag * frag_rate[...]
    for at_row, matrix in ((0, coag_full), (BINS, frag_full)):
        for kept, value in ((forth, matrix), (back, matrix.T)):
            hi, lo = high_low(value)
            kept[at_row : at_row + BINS, 0:BINS] = hi
            kept[at_row : at_row + BINS, BINS : 2 * BINS] = hi
            kept[at_row : at_row + BINS, 2 * BINS : 3 * BINS] = lo

    sigma = 1.0 / (1.0 + jnp.exp(-((speed[...] - frag_speed[...]) / GATE_WIDTH)))
    flagged = regime[...].astype(F32)
    gate_all = flagged * sigma
    slope_all = -flagged * sigma * (1.0 - sigma) / GATE_WIDTH
    block8 = lanes_of((ROWS, LANES)) // 32
    for source, kept in ((gate_all, gates), (slope_all, slopes)):
        value = jnp.zeros((ROWS, LANES), F32)
        for al in range(4):
            part = pltpu.roll(source[al * 8 : al * 8 + 8], lax.rem(32 * (al + MASS - m), LANES), 1)
            value = jnp.where(block8 == al, part, value)
        kept[...] = value

    for i in range(4):
        edge_copy(2, i).wait_recv()
    here[0] = edge_in[2, 2]
    here[33] = edge_in[2, 3]
    row_has_left = jnp.where(row > 0, 1.0, 0.0)
    row_has_right = jnp.where(row < rows - 1, 1.0, 0.0)

    def own_forward(i, carry):
        last_col, first_col = carry
        for k in range(4):
            a = i * 4 + k
            value = here[a + 1]
            beside = here[a] + here[a + 2]
            outer = jnp.where(topmost, rolled(first_col, k), rolled(in_q[...] * value, -1))
            inner = jnp.where(lowest, rolled(last_col, -k), rolled(out_q[...] * value, 1))
            there[a] = own_coef[0] * value + outer + inner + own_coef[1] * beside
        return rolled(last_col, -4), rolled(first_col, 4)

    lax.fori_loop(
        0,
        8,
        own_forward,
        (rolled(edge_in[2, 0], 32) * row_has_left, rolled(edge_in[2, 1], 96) * row_has_right),
    )

    def pack_m1(ah, carry):
        tiles = swap_blocks([there[al * 8 + ah] for al in range(4)])
        for k in range(MASS):
            pack_d[k, ah] = tiles[k]
        m1[ah, own] = pack_d[m, ah]
        return carry

    lax.fori_loop(0, ROWS, pack_m1, 0)

    def send_m1(i, carry):
        for k in (1, 2, 3):
            m1_copy(k, lax.rem(i + 7, 8)).start()
        return carry

    lax.fori_loop(0, EARLY, send_m1, 0)

    has_left = jnp.where(radial > 0, 1.0, 0.0)
    has_right = jnp.where(radial < radials - 1, 1.0, 0.0)

    def mix(n, source, matrix, way, state, arrive, seen):
        edge_out[n, 0] = zero
        edge_out[n, 1] = zero

        def body(j, carry):
            pair = (lax.rem(2 * j + 7, 8), 2 * j)
            for ah in pair:
                arrive(ah)
            x = jnp.concatenate([source[ah] for ah in pair], axis=1)
            x_hi, x_lo = high_low(x)
            xc = jnp.concatenate([x_hi, x_lo, x_hi], axis=0)
            gate = jnp.concatenate([gates[pl.ds(ah, 1)] for ah in pair], axis=1)
            news = []
            yfs = []
            for c in range(2):
                part = slice(c * 128, c * 128 + 128)
                yf = jnp.dot(matrix[BINS + c * 128 : BINS + c * 128 + 128], xc, preferred_element_type=F32)
                news.append(x[part] + jnp.dot(matrix[part], xc, preferred_element_type=F32) + gate * yf)
                yfs.append(yf)
            new = jnp.concatenate(news, axis=0)
            frags = jnp.concatenate(yfs, axis=0)
            last_col = rolled(edge_out[n, 0], -8)
            first_col = rolled(edge_out[n, 1], 8)
            for half, ah in enumerate(pair):
                lanes = slice(half * LANES, (half + 1) * LANES)
                state[ah + 1] = new[:, lanes]
                seen(ah, x[:, lanes], frags[:, lanes])
                for g in range(MASS):
                    bins = slice(g * RANGE, (g + 1) * RANGE)
                    value = new[bins, lanes]
                    to_left = value * coef[0, bins] if way == FORTH else value
                    to_right = value * coef[1, bins] if way == FORTH else value
                    u = half * MASS + g
                    last_col = jnp.where(within == 24 + u, rolled(to_right, u - 7), last_col)
                    first_col = jnp.where(within == 7 - u, rolled(to_left, 7 - u), first_col)
            edge_out[n, 0] = last_col
            edge_out[n, 1] = first_col

            @pl.when(j == 0)
            def _():
                for i, ah in ((2, ROWS), (3, 1)):
                    value = zero
                    for g in range(MASS):
                        bins = slice(g * RANGE, (g + 1) * RANGE)
                        part = rolled(state[ah, bins], 32 * (g - 3) if i == 2 else 32 * g)
                        value = jnp.where(block == g, part, value)
                    edge_out[n, i] = value
                    edge_copy(n, i).start()

            return carry

        lax.fori_loop(0, ROWS // 2, body, 0)
        edge_copy(n, 0).start()
        edge_copy(n, 1).start()

    def stencil(n, field, way, emit, after_row=None):
        edge_copy(n, 0).wait_recv()
        edge_copy(n, 1).wait_recv()

        def body(i, carry):
            last_col, first_col = carry
            ah = lax.rem(14 - i, 8)
            for t in range(MASS):
                g = MASS - 1 - t
                bins = slice(g * RANGE, (g + 1) * RANGE)
                value = field[ah + 1, bins]
                beside = field[ah, bins] + field[ah + 2, bins]
                c_in, c_out = coef[0, bins], coef[1, bins]
                to_left = c_in * value if way == FORTH else value
                to_right = c_out * value if way == FORTH else value
                outer = rolled(jnp.where(first, rolled(first_col, -t), to_left), -1)
                inner = rolled(jnp.where(final, rolled(last_col, t), to_right), 1)
                both = outer + inner if way == FORTH else c_in * inner + c_out * outer
                emit(ah, bins, coef[3, bins] * value + both + coef[2, bins] * beside)
            last_col = rolled(last_col, MASS)
            first_col = rolled(first_col, -MASS)
            if after_row is not None:
                after_row(ah)
            return last_col, first_col

        carry = (rolled(edge_in[n, 0], -32) * has_left, rolled(edge_in[n, 1], 32) * has_right)
        carry = lax.fori_loop(0, 6, body, carry)
        edge_copy(n, 2).wait_recv()
        edge_copy(n, 3).wait_recv()
        for g in range(MASS):
            bins = slice(g * RANGE, (g + 1) * RANGE)
            field[0, bins] = jnp.where(
                block == 0, rolled(edge_in[n, 2], -32 * g), rolled(field[ROWS, bins], 32)
            )
            field[ROWS + 1, bins] = jnp.where(
                block == 3, rolled(edge_in[n, 3], 32 * (3 - g)), rolled(field[1, bins], -32)
            )
        lax.fori_loop(6, 8, body, carry)

    def add_product(ah, value, other):
        summed = jnp.sum((value * other).reshape(-1, 8, LANES), axis=0)
        acc[...] += slopes[pl.ds(ah, 1)] * summed

    def arrived(copy):
        def wait(ah):
            for k in (1, 2, 3):
                copy(k, ah).wait_recv()

        return wait

    acc[...] = jnp.zeros((8, LANES), F32)

    def keep_f2(ah, x, frags):
        f2[ah] = frags

    mix(0, cot, back, BACK, w2, arrived(cot_copy), keep_f2)
    lax.fori_loop(EARLY, ROWS, send_m1, 0)

    for k in range(1, 8):
        share_copy(k).wait_recv()
    for g in range(MASS):
        bins = slice(g * RANGE, (g + 1) * RANGE)
        sent = jnp.concatenate([coef_all[i, g] for i in range(8)], axis=0)
        turns = [rolled(sent, 32 * k) for k in range(4)]

        def everywhere(source):
            value = turns[(0 - source) % 4]
            for b in (1, 2, 3):
                value = jnp.where(block == b, turns[(b - source) % 4], value)
            return value

        c_in, c_out, c_spread = everywhere(0), everywhere(1), everywhere(2)
        coef[0, bins] = c_in
        coef[1, bins] = c_out
        coef[2, bins] = c_spread
        coef[3, bins] = 1.0 - c_in - c_out - 2.0 * c_spread

    def keep_a1(ah, bins, value):
        a1[ah, bins] = value

    stencil(0, w2, BACK, keep_a1)

    def keep_f1(ah, x, frags):
        f1[ah] = frags

    mix(1, a1, back, BACK, w1, lambda ah: None, keep_f1)

    def first_product(ah, x, frags):
        add_product(ah, x, f1[ah])

    mix(3, m1, forth, FORTH, st, arrived(m1_copy), first_product)

    def keep_res(ah, bins, value):
        res[ah, bins] = value

    def send_row(ah):
        for k in (1, 2, 3):
            ret_copy(k, ah).start()
        ret[m, ah] = res[ah, own]

    stencil(1, w1, BACK, keep_res, send_row)

    def second_product(ah, bins, value):
        add_product(ah, value, f2[ah, bins])

    stencil(3, st, FORTH, second_product)

    flat_out = out.reshape(RANGE * 32, LANES)

    def unpack(i, carry):
        ah = lax.rem(14 - i, 8)
        arrived(ret_copy)(ah)
        tiles = swap_blocks([ret[k, ah] for k in range(MASS)])
        for al in range(4):
            flat_out[pl.ds(al * 8 + ah, RANGE, stride=32), :] = tiles[al]
        return carry

    total = jnp.sum(acc[...], axis=0, keepdims=True)
    total = total + rolled(total, 32) + rolled(total, 64) + rolled(total, 96)
    total = jnp.broadcast_to(total, (8, LANES))
    total = jnp.where(block8 == m, total, 0.0)
    for n, (place, peer) in enumerate(((low, low_peer), (corner, corner_peer))):
        red[n, place] = total
        copies = []
        for k in range(1, 8):
            copies.append(
                pltpu.make_async_remote_copy(
                    src_ref=red.at[n, place],
                    dst_ref=red.at[n, place],
                    send_sem=red_send.at[n, k - 1],
                    recv_sem=red_recv.at[n, k - 1],
                    device_id=peer(k),
                    device_id_type=MESH,
                )
            )
        for copy in copies:
            copy.start()
        lax.fori_loop(4 * n, 4 * n + 4, unpack, 0)
        for copy in copies:
            copy.wait()
        total = ((red[n, 0] + red[n, 1]) + (red[n, 2] + red[n, 3])) + (
            (red[n, 4] + red[n, 5]) + (red[n, 6] + red[n, 7])
        )
    grad[...] = total[0:1]

    def drain(ah, carry):
        for copy in (cot_copy, m1_copy, ret_copy):
            for k in (1, 2, 3):
                copy(k, ah).wait_send()
        return carry

    lax.fori_loop(0, ROWS, drain, 0)
    for k in (1, 2, 3):
        coef_copy(k).wait_send()
    for k in range(1, 8):
        share_copy(k).wait_send()
    for n in range(4):
        for i in range(4):
            edge_copy(n, i).wait_send()


def per_device(
    density,
    cotangent,
    drift_in,
    drift_out,
    spread,
    dest_bins,
    bott_split,
    coag_rate,
    frag_pairs,
    frag_gain,
    frag_rate,
    collide_speed,
    frag_speed,
    regime,
):
    keep = lambda v: pltpu.with_memory_space_constraint(v, pltpu.HBM)
    vmem = pl.BlockSpec(memory_space=pltpu.VMEM)
    hbm = pl.BlockSpec(memory_space=pltpu.HBM)
    field = pltpu.VMEM((ROWS, BINS, LANES), F32)
    padded = pltpu.VMEM((ROWS + 2, BINS, LANES), F32)
    packed = pltpu.VMEM((MASS, ROWS, RANGE, LANES), F32)
    raw = pltpu.VMEM(density.shape, F32)
    matrix = pltpu.VMEM((2 * BINS, 3 * BINS), BF16)
    small = pltpu.VMEM((ROWS, LANES), F32)
    edges = pltpu.VMEM((4, 4, RANGE, LANES), F32)
    tile = pltpu.VMEM((RANGE, LANES), F32)
    per_bin = pltpu.VMEM((1, BINS), F32)
    cells = pltpu.VMEM((32, LANES), F32)
    dma = pltpu.SemaphoreType.DMA
    adjoint, gradient = pl.pallas_call(
        kernel,
        out_shape=(
            jax.ShapeDtypeStruct(density.shape, F32),
            jax.ShapeDtypeStruct((1, LANES), F32),
        ),
        in_specs=[hbm] * 14,
        out_specs=(vmem, vmem),
        scratch_shapes=[
            pltpu.SMEM((MASS, MASS), jnp.int32),
            raw,
            raw,
            tile,
            tile,
            pltpu.VMEM((1, RANGE), F32),
            pltpu.VMEM((1, BINS), jnp.int32),
            per_bin,
            per_bin,
            pltpu.VMEM((BINS, BINS), F32),
            per_bin,
            cells,
            pltpu.VMEM((1, LANES), F32),
            pltpu.VMEM((32, LANES), jnp.int32),
            pltpu.VMEM((34, RANGE, LANES), F32),
            pltpu.VMEM((2, RANGE, LANES), F32),
            pltpu.VMEM((32, RANGE, LANES), F32),
            packed,
            packed,
            field,
            field,
            pltpu.VMEM((MASS, RANGE, LANES), F32),
            pltpu.VMEM((MASS, 8, LANES), F32),
            pltpu.VMEM((8, MASS, 8, LANES), F32),
            pltpu.VMEM((4, BINS, LANES), F32),
            matrix,
            matrix,
            small,
            small,
            padded,
            field,
            field,
            padded,
            field,
            padded,
            field,
            packed,
            edges,
            edges,
            small,
            pltpu.VMEM((2, 8, ROWS, LANES), F32),
            dma((14,)),
            dma((3, 3, ROWS)),
            dma((3, 3, ROWS)),
            dma((3,)),
            dma((3,)),
            dma((7,)),
            dma((7,)),
            dma((4, 4)),
            dma((4, 4)),
            dma((2, 7)),
            dma((2, 7)),
        ],
        compiler_params=pltpu.CompilerParams(
            collective_id=0, has_side_effects=True, vmem_limit_bytes=48 << 20
        ),
    )(keep(frag_pairs), keep(density), keep(cotangent), keep(drift_in), keep(drift_out), keep(spread[None, :]), keep(dest_bins[None, :]), keep(bott_split[None, :]), keep(coag_rate[None, :]), keep(frag_gain), keep(frag_rate[None, :]), keep(collide_speed), keep(frag_speed[None, :]), keep(regime))
    return adjoint, gradient[0]


def solution(mesh):
    in_specs = (
        P("mass", "phi", "row"),
        P("mass", "phi", "row"),
        P("mass", None),
        P("mass", None),
        P("mass"),
        P(),
        P(),
        P(),
        P(),
        P(),
        P(),
        P("phi", "row"),
        P("row"),
        P("phi", "row"),
    )
    out_specs = (P("mass", "phi", "row"), P("row"))
    return jax.shard_map(
        per_device, mesh=mesh, in_specs=in_specs, out_specs=out_specs, check_vma=False
    )
```

```python
import functools

import jax
import jax.numpy as jnp
from jax import lax
from jax.experimental import pallas as pl
from jax.experimental.pallas import tpu as pltpu
from jax.sharding import PartitionSpec as P


MESH = pl.DeviceIdType.MESH
F32 = jnp.float32
BF16 = jnp.bfloat16
RANGE = 64
MASS = 4
ROWS = 8
BINS = 256
LANES = 128
GATE_WIDTH = 0.5
BACK, FORTH = 0, 1
EARLY = 2


def lanes_of(shape):
    return lax.broadcasted_iota(jnp.int32, shape, len(shape) - 1)


def rolled(value, shift):
    shift = shift % LANES
    return value if shift == 0 else pltpu.roll(value, shift, value.ndim - 1)


def swap_blocks(tiles):
    block = lanes_of(tiles[0].shape) // 32
    low = block < 2
    even = block % 2 == 0
    s0, s1, s2, s3 = tiles
    a0 = jnp.where(low, s0, rolled(s2, 64))
    a2 = jnp.where(low, rolled(s0, 64), s2)
    a1 = jnp.where(low, s1, rolled(s3, 64))
    a3 = jnp.where(low, rolled(s1, 64), s3)
    return (
        jnp.where(even, a0, rolled(a1, 32)),
        jnp.where(even, rolled(a0, 96), a1),
        jnp.where(even, a2, rolled(a3, 32)),
        jnp.where(even, rolled(a2, 96), a3),
    )


def high_low(value):
    high = value.astype(BF16)
    return high, (value - high.astype(F32)).astype(BF16)


def kernel(
    pairs_hbm,
    density,
    cotangent,
    drift_in,
    drift_out,
    spread_hbm,
    dest_hbm,
    split_hbm,
    rate_hbm,
    gain_hbm,
    frag_rate_hbm,
    speed_hbm,
    frag_speed_hbm,
    regime_hbm,
    out,
    grad,
    pairs,
    raw_c,
    raw_d,
    in_q,
    out_q,
    spread,
    dest,
    split,
    rate,
    gain,
    frag_rate,
    speed,
    frag_speed,
    regime,
    here,
    own_coef,
    there,
    pack_c,
    pack_d,
    cot,
    m1,
    coef_out,
    coef_part,
    coef_all,
    coef,
    back,
    forth,
    gates,
    slopes,
    w2,
    f2,
    a1,
    w1,
    f1,
    st,
    res,
    ret,
    edge_out,
    edge_in,
    acc,
    red,
    load_sem,
    field_send,
    field_recv,
    coef_send,
    coef_recv,
    share_send,
    share_recv,
    edge_send,
    edge_recv,
    red_send,
    red_recv,
):
    phi = lax.axis_index("phi")
    row = lax.axis_index("row")
    m = lax.axis_index("mass")
    phis = lax.axis_size("phi")
    rows = lax.axis_size("row")
    low = lax.rem(phi, 8)
    high = phi // 8
    corner = high * MASS + m

    at = pl.multiple_of(row * LANES, LANES)
    sources = (
        (cotangent, raw_c),
        (spread_hbm, spread),
        (drift_in.at[:, pl.ds(at, LANES)], in_q),
        (drift_out.at[:, pl.ds(at, LANES)], out_q),
        (density, raw_d),
        (dest_hbm, dest),
        (split_hbm, split),
        (rate_hbm, rate),
        (gain_hbm, gain),
        (frag_rate_hbm, frag_rate),
        (pairs_hbm, pairs),
        (speed_hbm, speed),
        (frag_speed_hbm, frag_speed),
        (regime_hbm, regime),
    )
    loads = [pltpu.make_async_copy(x, y, load_sem.at[i]) for i, (x, y) in enumerate(sources)]
    for load in loads[:4]:
        load.start()

    def mass_peer(k):
        return {"mass": lax.rem(m + k, MASS)}

    def low_peer(k):
        return {"phi": high * 8 + lax.rem(low + k, 8)}

    def corner_peer(k):
        other = lax.rem(corner + k, 8)
        return {"phi": (other // MASS) * 8 + low, "mass": lax.rem(other, MASS)}

    radial = row * MASS + m
    radials = rows * MASS
    right_at = lax.rem(radial + 1, radials)
    left_at = lax.rem(radial + radials - 1, radials)
    right = {"row": right_at // MASS, "mass": lax.rem(right_at, MASS)}
    left = {"row": left_at // MASS, "mass": lax.rem(left_at, MASS)}
    row_right = {"row": lax.rem(row + 1, rows)}
    row_left = {"row": lax.rem(row + rows - 1, rows)}
    after = {"phi": lax.rem(phi + 1, phis)}
    before = {"phi": lax.rem(phi + phis - 1, phis)}

    barrier = pltpu.get_barrier_semaphore()
    greeted = [mass_peer(k) for k in (1, 2, 3)]
    greeted += [right, left, row_right, row_left, after, before]
    greeted += [low_peer(k) for k in range(1, 8)] + [corner_peer(k) for k in range(1, 8)]
    for device in greeted:
        pl.semaphore_signal(barrier, inc=1, device_id=device, device_id_type=MESH)

    tile = (RANGE, LANES)
    lane = lanes_of(tile)
    block = lane // 32
    within = lax.rem(lane, 32)
    first = within == 0
    final = within == 31
    zero = jnp.zeros(tile, F32)

    def field_copy(kind, k, ah, source, target):
        return pltpu.make_async_remote_copy(
            src_ref=source,
            dst_ref=target,
            send_sem=field_send.at[kind, k - 1, ah],
            recv_sem=field_recv.at[kind, k - 1, ah],
            device_id=mass_peer(k),
            device_id_type=MESH,
        )

    own = pl.ds(pl.multiple_of(m * RANGE, RANGE), RANGE)

    def cot_copy(k, ah):
        return field_copy(0, k, ah, pack_c.at[lax.rem(m + k, MASS), ah], cot.at[ah, own])

    def m1_copy(k, ah):
        return field_copy(1, k, ah, pack_d.at[lax.rem(m + k, MASS), ah], m1.at[ah, own])

    def ret_copy(k, ah):
        theirs = pl.ds(pl.multiple_of(lax.rem(m + k, MASS) * RANGE, RANGE), RANGE)
        return field_copy(2, k, ah, res.at[ah, theirs], ret.at[m, ah])

    eighth = pl.ds(pl.multiple_of(low * 8, 8), 8)

    def coef_copy(k):
        return pltpu.make_async_remote_copy(
            src_ref=coef_out.at[lax.rem(m + k, MASS), eighth],
            dst_ref=coef_part.at[m],
            send_sem=coef_send.at[k - 1],
            recv_sem=coef_recv.at[k - 1],
            device_id=mass_peer(k),
            device_id_type=MESH,
        )

    def share_copy(k):
        return pltpu.make_async_remote_copy(
            src_ref=coef_part,
            dst_ref=coef_all.at[low],
            send_sem=share_send.at[k - 1],
            recv_sem=share_recv.at[k - 1],
            device_id=low_peer(k),
            device_id_type=MESH,
        )

    def edge_copy(n, i):
        device = ((row_right, row_left) if n == 2 else (right, left)) + (after, before)
        return pltpu.make_async_remote_copy(
            src_ref=edge_out.at[n, i],
            dst_ref=edge_in.at[n, i],
            send_sem=edge_send.at[n, i],
            recv_sem=edge_recv.at[n, i],
            device_id=device[i],
            device_id_type=MESH,
        )

    for i in (1, 2, 3):
        loads[i].wait()
    square = (RANGE, RANGE)
    on_diag = lax.broadcasted_iota(jnp.int32, square, 0) == lanes_of(square)
    spread_col = jnp.sum(jnp.where(on_diag, jnp.broadcast_to(spread[...], square), 0.0), axis=1, keepdims=True)
    spread_tile = jnp.broadcast_to(spread_col, tile)
    for k in range(MASS):
        coef_out[k] = jnp.where(
            block == 0,
            rolled(in_q[...], -32 * k),
            jnp.where(block == 1, rolled(out_q[...], 32 - 32 * k), spread_tile),
        )
    coef_part[m] = coef_out[m, eighth]
    own_coef[0] = 1.0 - in_q[...] - out_q[...] - 2.0 * spread_tile
    own_coef[1] = spread_tile

    flat_c = raw_c.reshape(RANGE * 32, LANES)

    def send_cot(i, carry):
        ah = lax.rem(i + 7, 8)
        tiles = swap_blocks([flat_c[pl.ds(al * 8 + ah, RANGE, stride=32), :] for al in range(4)])
        for k in range(MASS):
            pack_c[k, ah] = tiles[k]
        for k in (1, 2, 3):
            cot_copy(k, ah).start()
        cot[ah, own] = pack_c[m, ah]
        return carry

    loads[0].wait()
    for load in loads[4:]:
        load.start()
    pl.semaphore_wait(barrier, len(greeted))
    for k in (1, 2, 3):
        coef_copy(k).start()
    lax.fori_loop(0, ROWS, send_cot, 0)

    loads[4].wait()
    flat_d = raw_d.reshape(RANGE * 32, LANES)
    edge_out[2, 2] = flat_d[pl.ds(31, RANGE, stride=32), :]
    edge_out[2, 3] = flat_d[pl.ds(0, RANGE, stride=32), :]
    edge_copy(2, 2).start()
    edge_copy(2, 3).start()
    lowest = lane == 0
    topmost = lane == LANES - 1

    def own_edges(i, carry):
        last_col, first_col = rolled(carry[0], -4), rolled(carry[1], 4)
        for k in range(4):
            a = i * 4 + k
            value = flat_d[pl.ds(a, RANGE, stride=32), :]
            here[a + 1] = value
            last_col = jnp.where(lane == LANES - 4 + k, rolled(out_q[...] * value, k - 3), last_col)
            first_col = jnp.where(lane == 3 - k, rolled(in_q[...] * value, 3 - k), first_col)
        return last_col, first_col

    last_col, first_col = lax.fori_loop(0, 8, own_edges, (zero, zero))
    edge_out[2, 0] = last_col
    edge_out[2, 1] = first_col
    edge_copy(2, 0).start()
    edge_copy(2, 1).start()
    for k in (1, 2, 3):
        coef_copy(k).wait_recv()
    for k in range(1, 8):
        share_copy(k).start()
    coef_all[low] = coef_part[...]

    for load in loads[5:]:
        load.wait()
    whole = (BINS, BINS)
    row_ids = lax.broadcasted_iota(jnp.int32, whole, 0)
    col_ids = lanes_of(whole)
    target = jnp.broadcast_to(dest[...], whole)
    upper = jnp.broadcast_to(split[...], whole)
    diag = jnp.where(row_ids == col_ids, 1.0, 0.0)
    coag_full = (
        jnp.where(row_ids == target, 1.0 - upper, 0.0) + jnp.where(row_ids == target + 1, upper, 0.0) - diag
    ) * rate[...]
    strip = (RANGE, BINS)
    strip_block = lanes_of(strip) // RANGE
    chosen = []
    for i in range(MASS):
        line = jnp.zeros(strip, F32)
        for j in range(MASS):
            line = jnp.where(strip_block == j, pairs[i, j].astype(F32), line)
        chosen.append(line)
    chosen = jnp.concatenate(chosen, axis=0)
    frag_full = gain[...] * chosen * jnp.where(row_ids <= col_ids, 1.0, 0.0) - diag * frag_rate[...]
    for at_row, matrix in ((0, coag_full), (BINS, frag_full)):
        for kept, value in ((forth, matrix), (back, matrix.T)):
            hi, lo = high_low(value)
            kept[at_row : at_row + BINS, 0:BINS] = hi
            kept[at_row : at_row + BINS, BINS : 2 * BINS] = hi
            kept[at_row : at_row + BINS, 2 * BINS : 3 * BINS] = lo

    sigma = 1.0 / (1.0 + jnp.exp(-((speed[...] - frag_speed[...]) / GATE_WIDTH)))
    flagged = regime[...].astype(F32)
    gate_all = flagged * sigma
    slope_all = -flagged * sigma * (1.0 - sigma) / GATE_WIDTH
    block8 = lanes_of((ROWS, LANES)) // 32
    for source, kept in ((gate_all, gates), (slope_all, slopes)):
        value = jnp.zeros((ROWS, LANES), F32)
        for al in range(4):
            part = pltpu.roll(source[al * 8 : al * 8 + 8], lax.rem(32 * (al + MASS - m), LANES), 1)
            value = jnp.where(block8 == al, part, value)
        kept[...] = value

    for i in range(4):
        edge_copy(2, i).wait_recv()
    here[0] = edge_in[2, 2]
    here[33] = edge_in[2, 3]
    row_has_left = jnp.where(row > 0, 1.0, 0.0)
    row_has_right = jnp.where(row < rows - 1, 1.0, 0.0)

    def own_forward(i, carry):
        last_col, first_col = carry
        for k in range(4):
            a = i * 4 + k
            value = here[a + 1]
            beside = here[a] + here[a + 2]
            outer = jnp.where(topmost, rolled(first_col, k), rolled(in_q[...] * value, -1))
            inner = jnp.where(lowest, rolled(last_col, -k), rolled(out_q[...] * value, 1))
            there[a] = own_coef[0] * value + outer + inner + own_coef[1] * beside
        return rolled(last_col, -4), rolled(first_col, 4)

    lax.fori_loop(
        0,
        8,
        own_forward,
        (rolled(edge_in[2, 0], 32) * row_has_left, rolled(edge_in[2, 1], 96) * row_has_right),
    )

    def pack_m1(ah, carry):
        tiles = swap_blocks([there[al * 8 + ah] for al in range(4)])
        for k in range(MASS):
            pack_d[k, ah] = tiles[k]
        m1[ah, own] = pack_d[m, ah]
        return carry

    lax.fori_loop(0, ROWS, pack_m1, 0)

    def send_m1(i, carry):
        for k in (1, 2, 3):
            m1_copy(k, lax.rem(i + 7, 8)).start()
        return carry

    lax.fori_loop(0, EARLY, send_m1, 0)

    has_left = jnp.where(radial > 0, 1.0, 0.0)
    has_right = jnp.where(radial < radials - 1, 1.0, 0.0)

    def mix(n, source, matrix, way, state, arrive, seen):
        edge_out[n, 0] = zero
        edge_out[n, 1] = zero

        def body(j, carry):
            pair = (lax.rem(2 * j + 7, 8), 2 * j)
            for ah in pair:
                arrive(ah)
            x = jnp.concatenate([source[ah] for ah in pair], axis=1)
            x_hi, x_lo = high_low(x)
            xc = jnp.concatenate([x_hi, x_lo, x_hi], axis=0)
            gate = jnp.concatenate([gates[pl.ds(ah, 1)] for ah in pair], axis=1)
            news = []
            yfs = []
            for c in range(2):
                part = slice(c * 128, c * 128 + 128)
                yf = jnp.dot(matrix[BINS + c * 128 : BINS + c * 128 + 128], xc, preferred_element_type=F32)
                news.append(x[part] + jnp.dot(matrix[part], xc, preferred_element_type=F32) + gate * yf)
                yfs.append(yf)
            new = jnp.concatenate(news, axis=0)
            frags = jnp.concatenate(yfs, axis=0)
            last_col = rolled(edge_out[n, 0], -8)
            first_col = rolled(edge_out[n, 1], 8)
            for half, ah in enumerate(pair):
                lanes = slice(half * LANES, (half + 1) * LANES)
                state[ah + 1] = new[:, lanes]
                seen(ah, x[:, lanes], frags[:, lanes])
                for g in range(MASS):
                    bins = slice(g * RANGE, (g + 1) * RANGE)
                    value = new[bins, lanes]
                    to_left = value * coef[0, bins] if way == FORTH else value
                    to_right = value * coef[1, bins] if way == FORTH else value
                    u = half * MASS + g
                    last_col = jnp.where(within == 24 + u, rolled(to_right, u - 7), last_col)
                    first_col = jnp.where(within == 7 - u, rolled(to_left, 7 - u), first_col)
            edge_out[n, 0] = last_col
            edge_out[n, 1] = first_col

            @pl.when(j == 0)
            def _():
                for i, ah in ((2, ROWS), (3, 1)):
                    value = zero
                    for g in range(MASS):
                        bins = slice(g * RANGE, (g + 1) * RANGE)
                        part = rolled(state[ah, bins], 32 * (g - 3) if i == 2 else 32 * g)
                        value = jnp.where(block == g, part, value)
                    edge_out[n, i] = value
                    edge_copy(n, i).start()

            return carry

        lax.fori_loop(0, ROWS // 2, body, 0)
        edge_copy(n, 0).start()
        edge_copy(n, 1).start()

    def stencil(n, field, way, emit, after_row=None):
        edge_copy(n, 0).wait_recv()
        edge_copy(n, 1).wait_recv()

        def body(i, carry):
            last_col, first_col = carry
            ah = lax.rem(14 - i, 8)
            for t in range(MASS):
                g = MASS - 1 - t
                bins = slice(g * RANGE, (g + 1) * RANGE)
                value = field[ah + 1, bins]
                beside = field[ah, bins] + field[ah + 2, bins]
                c_in, c_out = coef[0, bins], coef[1, bins]
                to_left = c_in * value if way == FORTH else value
                to_right = c_out * value if way == FORTH else value
                outer = rolled(jnp.where(first, rolled(first_col, -t), to_left), -1)
                inner = rolled(jnp.where(final, rolled(last_col, t), to_right), 1)
                both = outer + inner if way == FORTH else c_in * inner + c_out * outer
                emit(ah, bins, coef[3, bins] * value + both + coef[2, bins] * beside)
            last_col = rolled(last_col, MASS)
            first_col = rolled(first_col, -MASS)
            if after_row is not None:
                after_row(ah)
            return last_col, first_col

        carry = (rolled(edge_in[n, 0], -32) * has_left, rolled(edge_in[n, 1], 32) * has_right)
        carry = lax.fori_loop(0, 6, body, carry)
        edge_copy(n, 2).wait_recv()
        edge_copy(n, 3).wait_recv()
        for g in range(MASS):
            bins = slice(g * RANGE, (g + 1) * RANGE)
            field[0, bins] = jnp.where(
                block == 0, rolled(edge_in[n, 2], -32 * g), rolled(field[ROWS, bins], 32)
            )
            field[ROWS + 1, bins] = jnp.where(
                block == 3, rolled(edge_in[n, 3], 32 * (3 - g)), rolled(field[1, bins], -32)
            )
        lax.fori_loop(6, 8, body, carry)

    def add_product(ah, value, other):
        summed = jnp.sum((value * other).reshape(-1, 8, LANES), axis=0)
        acc[...] += slopes[pl.ds(ah, 1)] * summed

    def arrived(copy):
        def wait(ah):
            for k in (1, 2, 3):
                copy(k, ah).wait_recv()

        return wait

    acc[...] = jnp.zeros((8, LANES), F32)

    def keep_f2(ah, x, frags):
        f2[ah] = frags

    mix(0, cot, back, BACK, w2, arrived(cot_copy), keep_f2)
    lax.fori_loop(EARLY, ROWS, send_m1, 0)

    for k in range(1, 8):
        share_copy(k).wait_recv()
    for g in range(MASS):
        bins = slice(g * RANGE, (g + 1) * RANGE)
        sent = jnp.concatenate([coef_all[i, g] for i in range(8)], axis=0)
        turns = [rolled(sent, 32 * k) for k in range(4)]

        def everywhere(source):
            value = turns[(0 - source) % 4]
            for b in (1, 2, 3):
                value = jnp.where(block == b, turns[(b - source) % 4], value)
            return value

        c_in, c_out, c_spread = everywhere(0), everywhere(1), everywhere(2)
        coef[0, bins] = c_in
        coef[1, bins] = c_out
        coef[2, bins] = c_spread
        coef[3, bins] = 1.0 - c_in - c_out - 2.0 * c_spread

    def keep_a1(ah, bins, value):
        a1[ah, bins] = value

    stencil(0, w2, BACK, keep_a1)

    def keep_f1(ah, x, frags):
        f1[ah] = frags

    mix(1, a1, back, BACK, w1, lambda ah: None, keep_f1)

    def first_product(ah, x, frags):
        @pl.when(jnp.logical_and(ah != 5, ah != 6))
        def _():
            add_product(ah, x, f1[ah])

    mix(3, m1, forth, FORTH, st, arrived(m1_copy), first_product)

    def keep_res(ah, bins, value):
        res[ah, bins] = value

    def send_row(ah):
        for k in (1, 2, 3):
            ret_copy(k, ah).start()
        ret[m, ah] = res[ah, own]

    stencil(1, w1, BACK, keep_res, send_row)

    for ah in (5, 6):
        add_product(ah, m1[ah], f1[ah])

    def second_product(ah, bins, value):
        add_product(ah, value, f2[ah, bins])

    stencil(3, st, FORTH, second_product)

    flat_out = out.reshape(RANGE * 32, LANES)

    def unpack(i, carry):
        ah = lax.rem(14 - i, 8)
        arrived(ret_copy)(ah)
        tiles = swap_blocks([ret[k, ah] for k in range(MASS)])
        for al in range(4):
            flat_out[pl.ds(al * 8 + ah, RANGE, stride=32), :] = tiles[al]
        return carry

    total = jnp.sum(acc[...], axis=0, keepdims=True)
    total = total + rolled(total, 32) + rolled(total, 64) + rolled(total, 96)
    total = jnp.broadcast_to(total, (8, LANES))
    total = jnp.where(block8 == m, total, 0.0)
    for n, (place, peer) in enumerate(((low, low_peer), (corner, corner_peer))):
        red[n, place] = total
        copies = []
        for k in range(1, 8):
            copies.append(
                pltpu.make_async_remote_copy(
                    src_ref=red.at[n, place],
                    dst_ref=red.at[n, place],
                    send_sem=red_send.at[n, k - 1],
                    recv_sem=red_recv.at[n, k - 1],
                    device_id=peer(k),
                    device_id_type=MESH,
                )
            )
        for copy in copies:
            copy.start()
        lax.fori_loop(4 * n, 4 * n + 4, unpack, 0)
        for copy in copies:
            copy.wait()
        total = ((red[n, 0] + red[n, 1]) + (red[n, 2] + red[n, 3])) + (
            (red[n, 4] + red[n, 5]) + (red[n, 6] + red[n, 7])
        )
    grad[...] = total[0:1]

    def drain(ah, carry):
        for copy in (cot_copy, m1_copy, ret_copy):
            for k in (1, 2, 3):
                copy(k, ah).wait_send()
        return carry

    lax.fori_loop(0, ROWS, drain, 0)
    for k in (1, 2, 3):
        coef_copy(k).wait_send()
    for k in range(1, 8):
        share_copy(k).wait_send()
    for n in range(4):
        for i in range(4):
            edge_copy(n, i).wait_send()


def per_device(
    density,
    cotangent,
    drift_in,
    drift_out,
    spread,
    dest_bins,
    bott_split,
    coag_rate,
    frag_pairs,
    frag_gain,
    frag_rate,
    collide_speed,
    frag_speed,
    regime,
):
    keep = lambda v: pltpu.with_memory_space_constraint(v, pltpu.HBM)
    vmem = pl.BlockSpec(memory_space=pltpu.VMEM)
    hbm = pl.BlockSpec(memory_space=pltpu.HBM)
    field = pltpu.VMEM((ROWS, BINS, LANES), F32)
    padded = pltpu.VMEM((ROWS + 2, BINS, LANES), F32)
    packed = pltpu.VMEM((MASS, ROWS, RANGE, LANES), F32)
    raw = pltpu.VMEM(density.shape, F32)
    matrix = pltpu.VMEM((2 * BINS, 3 * BINS), BF16)
    small = pltpu.VMEM((ROWS, LANES), F32)
    edges = pltpu.VMEM((4, 4, RANGE, LANES), F32)
    tile = pltpu.VMEM((RANGE, LANES), F32)
    per_bin = pltpu.VMEM((1, BINS), F32)
    cells = pltpu.VMEM((32, LANES), F32)
    dma = pltpu.SemaphoreType.DMA
    adjoint, gradient = pl.pallas_call(
        kernel,
        out_shape=(
            jax.ShapeDtypeStruct(density.shape, F32),
            jax.ShapeDtypeStruct((1, LANES), F32),
        ),
        in_specs=[hbm] * 14,
        out_specs=(vmem, vmem),
        scratch_shapes=[
            pltpu.SMEM((MASS, MASS), jnp.int32),
            raw,
            raw,
            tile,
            tile,
            pltpu.VMEM((1, RANGE), F32),
            pltpu.VMEM((1, BINS), jnp.int32),
            per_bin,
            per_bin,
            pltpu.VMEM((BINS, BINS), F32),
            per_bin,
            cells,
            pltpu.VMEM((1, LANES), F32),
            pltpu.VMEM((32, LANES), jnp.int32),
            pltpu.VMEM((34, RANGE, LANES), F32),
            pltpu.VMEM((2, RANGE, LANES), F32),
            pltpu.VMEM((32, RANGE, LANES), F32),
            packed,
            packed,
            field,
            field,
            pltpu.VMEM((MASS, RANGE, LANES), F32),
            pltpu.VMEM((MASS, 8, LANES), F32),
            pltpu.VMEM((8, MASS, 8, LANES), F32),
            pltpu.VMEM((4, BINS, LANES), F32),
            matrix,
            matrix,
            small,
            small,
            padded,
            field,
            field,
            padded,
            field,
            padded,
            field,
            packed,
            edges,
            edges,
            small,
            pltpu.VMEM((2, 8, ROWS, LANES), F32),
            dma((14,)),
            dma((3, 3, ROWS)),
            dma((3, 3, ROWS)),
            dma((3,)),
            dma((3,)),
            dma((7,)),
            dma((7,)),
            dma((4, 4)),
            dma((4, 4)),
            dma((2, 7)),
            dma((2, 7)),
        ],
        compiler_params=pltpu.CompilerParams(
            collective_id=0, has_side_effects=True, vmem_limit_bytes=48 << 20
        ),
    )(keep(frag_pairs), keep(density), keep(cotangent), keep(drift_in), keep(drift_out), keep(spread[None, :]), keep(dest_bins[None, :]), keep(bott_split[None, :]), keep(coag_rate[None, :]), keep(frag_gain), keep(frag_rate[None, :]), keep(collide_speed), keep(frag_speed[None, :]), keep(regime))
    return adjoint, gradient[0]


def solution(mesh):
    in_specs = (
        P("mass", "phi", "row"),
        P("mass", "phi", "row"),
        P("mass", None),
        P("mass", None),
        P("mass"),
        P(),
        P(),
        P(),
        P(),
        P(),
        P(),
        P("phi", "row"),
        P("row"),
        P("phi", "row"),
    )
    out_specs = (P("mass", "phi", "row"), P("row"))
    return jax.shard_map(
        per_device, mesh=mesh, in_specs=in_specs, out_specs=out_specs, check_vma=False
    )
```
